256 devices in a mesh: row: 8 (over x, core), col: 32 (over z, y).
Axes of the slice: x: 4, y: 4, z: 8, core: 2. Of those that a mesh axis runs over, the one named last changes fastest.
Arguments:
- pair_rep: bfloat16 [2048, 2048, 128], P('row', 'col'), may hold values from -6 to 6
- queries: bfloat16 [2048, 192], P(('row', 'col')), may hold values from -12 to 12
- qpoints: bfloat16 [2048, 144], P(('row', 'col')), may hold values from -6 to 6
- frames: float32 [2048, 12], P(('row', 'col')), may hold values from -4 to 4, as said below
- keyset: bfloat16 [2048, 192], P('col', 'row'), may hold values from -12 to 12
- kpoints: bfloat16 [2048, 144], P('col', 'row'), may hold values from -6 to 6
- values: bfloat16 [2048, 192], P('col', 'row'), may hold values from -6 to 6
- vpoints: bfloat16 [2048, 288], P('col', 'row'), may hold values from -6 to 6
- key_mask: int32 [2048], P('col'), may hold values 0 or 1
- bias_weight: bfloat16 [128, 12], replicated, may hold values from -0.5 to 0.5
- head_weight: float32 [12], replicated, may hold values from -1.5 to 1.5
- grad_scalar: bfloat16 [2048, 192], P(('row', 'col')), may hold values from -6 to 6
- grad_pair: bfloat16 [2048, 1536], P(('row', 'col')), may hold values from -6 to 6
- grad_points: bfloat16 [2048, 288], P(('row', 'col')), may hold values from -6 to 6
Outputs:
- pair_grad: bfloat16 [2048, 2048, 128], P('row', 'col')
- queries_grad: float32 [2048, 192], P(('row', 'col'))
- qpoints_grad: float32 [2048, 144], P(('row', 'col'))
- keyset_grad: float32 [2048, 192], P('col', 'row')
- kpoints_grad: float32 [2048, 144], P('col', 'row')
- values_grad: float32 [2048, 192], P('col', 'row')
- vpoints_grad: float32 [2048, 288], P('col', 'row')
- bias_grad: float32 [128, 12], replicated
- head_grad: float32 [12], replicated
The draws below stay inside these ranges and needn't reach their ends.
Inputs may be any that keep to these rules, and one draw needn't show every extreme that they name: `frames`: each row is a rotation matrix, row-major, followed by a translation.
All inputs are finite; a program needn't handle non-finite values. No bound on the sum of `key_mask` on one device may be relied on, other than what follows from the above.
Results may differ from the reference program's by a relative error of at most 0.023.
Values may be sent and summed in bfloat16 or wider, within the bound.
A program may use at most 64 MiB of HBM per device.

```python
import math
import jax
import jax.numpy as jnp
from jax import lax

H = 12
C = 16
CZ = 128
PQ = 4
PV = 8
N = 2048
LOSS = 128


def draw_queries(key, part):
    noise_key = jax.random.fold_in(key, 21)
    drawn = jnp.clip(jax.random.normal(noise_key, (N, H * C), jnp.float32), -12.0, 12.0)
    return drawn.astype(jnp.bfloat16)


def draw_keyset(key, part):
    noise_key = jax.random.fold_in(key, 31)
    drawn = jnp.clip(jax.random.normal(noise_key, (N, H * C), jnp.float32), -12.0, 12.0)
    return drawn.astype(jnp.bfloat16)


def draw_frames(key, part):
    quat = jax.random.normal(jax.random.fold_in(key, 41), (N, 4), jnp.float32)
    scalar_part = jnp.abs(quat[:, 0]) + 1.0
    length = jnp.sqrt(scalar_part * scalar_part + jnp.sum(quat[:, 1:] * quat[:, 1:], axis=1))
    real_w = scalar_part / length
    axis_x = quat[:, 1] / length
    axis_y = quat[:, 2] / length
    axis_z = quat[:, 3] / length
    entries = [1.0 - 2.0 * (axis_y * axis_y + axis_z * axis_z), 2.0 * (axis_x * axis_y - real_w * axis_z), 2.0 * (axis_x * axis_z + real_w * axis_y), 2.0 * (axis_x * axis_y + real_w * axis_z), 1.0 - 2.0 * (axis_x * axis_x + axis_z * axis_z), 2.0 * (axis_y * axis_z - real_w * axis_x), 2.0 * (axis_x * axis_z - real_w * axis_y), 2.0 * (axis_y * axis_z + real_w * axis_x), 1.0 - 2.0 * (axis_x * axis_x + axis_y * axis_y)]
    rotation = jnp.stack(entries, axis=1)
    translation = jnp.clip(1.5 * jax.random.normal(jax.random.fold_in(key, 42), (N, 3), jnp.float32), -4.0, 4.0)
    return jnp.concatenate([rotation, translation], axis=1).astype(jnp.float32)


def set_ends(values, key, least, top_value):
    extent = values.shape
    index_at = [jax.random.randint(jax.random.fold_in(key, axis), (), 0, extent[axis]) for axis in range(len(extent))]
    values = values.at[tuple(index_at)].set(least)
    longest = extent.index(max(extent))
    index_at[longest] = (index_at[longest] + 1) % extent[longest]
    return values.at[tuple(index_at)].set(top_value)


def levels(own_key, shape, split, low, largest):
    gain, own = 1.0, jax.random.fold_in(own_key, 6)
    for axis_at, blocks in split:
        draws = jnp.exp(jax.random.uniform(jax.random.fold_in(own, axis_at), (blocks,), jnp.float32, low / len(split), largest / len(split)))
        gain = gain * jnp.repeat(draws, shape[axis_at] // blocks).reshape([-1 if axis == axis_at else 1 for axis in range(len(shape))])
    return gain


def normal_values(stream_key, dims, scale, reach, shards=(), held_as=jnp.bfloat16):
    level = levels(stream_key, dims, shards, -0.22, 0.18) if shards else 1.0
    values = jax.random.normal(stream_key, dims, jnp.float32) * scale * level
    return jnp.minimum(jnp.maximum(values, -reach), reach).astype(held_as)


def setup_inputs(seed: int = 0) -> dict:
    seeds = jax.random.split(jax.random.key(seed), 15)
    return {
        "pair_rep": normal_values(seeds[0], (N, N, CZ), 1.0, 6.0, ((0, 8), (1, 32))),
        "queries": draw_queries(jax.random.fold_in(seeds[14], 71), 0),
        "qpoints": normal_values(seeds[2], (N, 3 * H * PQ), 1.0, 6.0, ((0, 256),)),
        "frames": draw_frames(jax.random.fold_in(seeds[14], 71), 0),
        "keyset": draw_keyset(jax.random.fold_in(seeds[14], 71), 0),
        "kpoints": normal_values(seeds[5], (N, 3 * H * PQ), 1.0, 6.0, ((0, 32), (1, 8))),
        "values": normal_values(seeds[6], (N, H * C), 1.0, 6.0, ((0, 32), (1, 8))),
        "vpoints": normal_values(seeds[7], (N, 3 * H * PV), 1.0, 6.0, ((0, 32), (1, 8))),
        "key_mask": set_ends((jax.random.randint(seeds[8], (N,), 0, 8) < 7).astype(jnp.int32), jax.random.fold_in(seeds[8], 1), 0, 1),
        "bias_weight": normal_values(seeds[9], (CZ, H), CZ ** -0.5, 0.5),
        "head_weight": jnp.clip(jax.random.uniform(seeds[10], (H,), jnp.float32, -1.5, 1.5), -1.5, 1.5),
        "grad_scalar": normal_values(seeds[11], (N, H * C), 1.0, 6.0, ((0, 256),)),
        "grad_pair": normal_values(seeds[12], (N, H * CZ), 1.0, 6.0, ((0, 256),)),
        "grad_points": normal_values(seeds[13], (N, 3 * H * PV), 1.0, 6.0, ((0, 256),)),
    }


def product(form, left, right):
    return jnp.einsum(form, left.astype(jnp.float32), right.astype(jnp.float32), precision=lax.Precision.HIGHEST)

def reference(pair_rep, queries, qpoints, frames, keyset, kpoints, values, vpoints, key_mask, bias_weight, head_weight, grad_scalar, grad_pair, grad_points):
    logit_weight = math.sqrt(1.0 / 3.0)
    point_weight = math.sqrt(2.0 / (9.0 * PQ))
    inv_width = 1.0 / math.sqrt(C)
    loss_scale = float(LOSS)
    rotation = frames[:, :9].reshape(N, 3, 3)
    translation = frames[:, 9:]
    query_glob = (product('nab,nhpb->nhpa', rotation, qpoints.reshape(N, H, PQ, 3)) + translation[:, None, None, :]).astype(jnp.bfloat16)
    grad_glob = product('nab,nhpb->nhpa', rotation, grad_points.astype(jnp.float32).reshape(N, H, PV, 3) * loss_scale).astype(jnp.bfloat16)
    grad_vecs = (grad_scalar.astype(jnp.float32) * loss_scale).astype(jnp.bfloat16).reshape(N, H, C)
    grad_pairs = (grad_pair.astype(jnp.float32) * loss_scale).astype(jnp.bfloat16).reshape(N, H, CZ)
    query_vecs = queries.reshape(N, H, C)
    point_gamma = jax.nn.softplus(head_weight)
    key_vecs = keyset.reshape(N, H, C)
    key_glob = kpoints.reshape(N, H, PQ, 3)
    value_vecs = values.reshape(N, H, C)
    value_glob = vpoints.reshape(N, H, PV, 3)
    key_square = lax.optimization_barrier(jnp.sum(jnp.square(key_glob.astype(jnp.float32)), axis=(2, 3)))
    masking = 100000.0 * (1.0 - key_mask.astype(jnp.float32))
    block_rows = min(128, N)
    block_count = N // block_rows
    dist_weight = 0.5 * logit_weight * point_weight

    def one_block(carried, block_index):
        first_row = block_index * block_rows

        def take_rows(array):
            return lax.dynamic_slice_in_dim(array, first_row, block_rows, 0)
        pair_block = take_rows(pair_rep)
        qvec_block = take_rows(query_vecs)
        qglob_block = take_rows(query_glob)
        gvec_block = take_rows(grad_vecs)
        gpair_block = take_rows(grad_pairs)
        gglob_block = take_rows(grad_glob)
        rot_block = take_rows(rotation)
        dot_terms = product('ihc,jhc->hij', qvec_block, key_vecs)
        bias = product('ijc,ch->hij', pair_block, bias_weight)
        cross_terms = product('ihpx,jhpx->hij', qglob_block, key_glob)
        query_square = lax.optimization_barrier(jnp.sum(jnp.square(qglob_block.astype(jnp.float32)), axis=(2, 3)))
        distance = query_square.T[:, :, None] + key_square.T[:, None, :] - 2.0 * cross_terms
        scores = logit_weight * (dot_terms * inv_width + bias) - dist_weight * point_gamma[:, None, None] * distance - masking[None, None, :]
        attention = jax.nn.softmax(scores, axis=-1)
        attention_half = attention.astype(jnp.bfloat16)
        prob_grad = product('ihc,jhc->hij', gvec_block, value_vecs) + product('ihc,ijc->hij', gpair_block, pair_block) + product('ihpx,jhpx->hij', gglob_block, value_glob)
        inner_sum = lax.optimization_barrier(jnp.sum(attention * prob_grad, axis=-1, keepdims=True))
        score_grad = attention * (prob_grad - inner_sum)
        score_half = score_grad.astype(jnp.bfloat16)
        rowsum = lax.optimization_barrier(jnp.sum(score_half.astype(jnp.float32), axis=2))
        colsum = lax.optimization_barrier(jnp.sum(score_half.astype(jnp.float32), axis=1))
        query_part = logit_weight * inv_width * product('hij,jhc->ihc', score_half, key_vecs)
        glob_part = logit_weight * point_weight * point_gamma[None, :, None, None] * (product('hij,jhpx->ihpx', score_half, key_glob) - qglob_block.astype(jnp.float32) * rowsum.T[:, :, None, None])
        anchor_part = product('nba,nhpb->nhpa', rot_block, glob_part)
        key_part = logit_weight * inv_width * product('hij,ihc->jhc', score_half, qvec_block)
        kpoint_part = logit_weight * point_weight * point_gamma[None, :, None, None] * (product('hij,ihpx->jhpx', score_half, qglob_block) - key_glob.astype(jnp.float32) * colsum.T[:, :, None, None])
        value_part = product('hij,ihc->jhc', attention_half, gvec_block)
        vpoint_part = product('hij,ihpx->jhpx', attention_half, gglob_block)
        pair_part = (logit_weight * product('hij,ch->ijc', score_half, bias_weight) + product('hij,ihc->ijc', attention_half, gpair_block)).astype(jnp.bfloat16)
        bias_part = logit_weight * product('ijc,hij->ch', pair_block, score_half)
        gamma_part = -dist_weight * lax.optimization_barrier(jnp.sum(score_grad * distance, axis=(1, 2)))
        updated = (carried[0] + key_part, carried[1] + kpoint_part, carried[2] + value_part, carried[3] + vpoint_part, carried[4] + bias_part, carried[5] + gamma_part)
        return (updated, (pair_part, query_part.reshape(block_rows, H * C), anchor_part.reshape(block_rows, 3 * H * PQ)))
    initial = (jnp.zeros((N, H, C), jnp.float32), jnp.zeros((N, H, PQ, 3), jnp.float32), jnp.zeros((N, H, C), jnp.float32), jnp.zeros((N, H, PV, 3), jnp.float32), jnp.zeros((CZ, H), jnp.float32), jnp.zeros((H,), jnp.float32))
    totals, stacked = lax.scan(one_block, initial, jnp.arange(block_count, dtype=jnp.int32))
    pair_grad = stacked[0].reshape(N, N, CZ)
    queries_grad = stacked[1].reshape(N, H * C)
    qpoints_grad = stacked[2].reshape(N, 3 * H * PQ)
    keyset_grad = totals[0].reshape(N, H * C)
    kpoints_grad = totals[1].reshape(N, 3 * H * PQ)
    values_grad = totals[2].reshape(N, H * C)
    vpoints_grad = totals[3].reshape(N, 3 * H * PV)
    bias_grad = totals[4] / float(N)
    head_grad = totals[5] * jax.nn.sigmoid(head_weight) / float(N)
    return (pair_grad, queries_grad, qpoints_grad, keyset_grad, kpoints_grad, values_grad, vpoints_grad, bias_grad, head_grad)
```

```python
import functools
import math

import jax
import jax.numpy as jnp
from jax import lax
from jax.experimental import pallas as pl
from jax.experimental.pallas import tpu as pltpu
from jax.sharding import PartitionSpec as P

H = 12
C = 16
CZ = 128
PQ = 4
PV = 8
LANES = 128
ROWS = 8
FEATURES = 1024
MESH = pl.DeviceIdType.MESH
F32 = jnp.float32
BF16 = jnp.bfloat16
WL = math.sqrt(1.0 / 3.0)
WC = math.sqrt(2.0 / (9.0 * PQ))
DIST_WEIGHT = 0.5 * WL * WC


def nt(a, b):
    return lax.dot_general(a, b, (((1,), (1,)), ((), ())), preferred_element_type=F32)


def nn(a, b):
    return lax.dot_general(a, b, (((1,), (0,)), ((), ())), preferred_element_type=F32)


def iota(shape, dim):
    return lax.broadcasted_iota(jnp.int32, shape, dim).astype(F32)


def whole_part(x, divisor):
    return jnp.floor((x + 0.5) * (1.0 / divisor))


def padded(scratch, array, width):
    rows, used = array.shape
    scratch[0:rows, 0:width] = jnp.zeros((rows, width), F32)
    scratch[0:rows, 0:used] = array.astype(F32)
    return scratch[0:rows, 0:width]


def rotated(frames, points, width, back):
    lane = iota((ROWS, width), 1)
    place = lane - 3.0 * whole_part(lane, 3)
    total = jnp.zeros((ROWS, width), F32)
    for step in range(-2, 3):
        factor = jnp.zeros((ROWS, width), F32)
        for a in range(3):
            b = a + step
            if 0 <= b < 3:
                at = 3 * b + a if back else 3 * a + b
                factor = jnp.where(place == float(a), frames[:, at : at + 1], factor)
        moved = points if step == 0 else pltpu.roll(points, (-step) % width, 1)
        total = total + factor * moved
    return total


def shifted(frames, width):
    lane = iota((ROWS, width), 1)
    place = lane - 3.0 * whole_part(lane, 3)
    total = jnp.zeros((ROWS, width), F32)
    for a in range(3):
        total = jnp.where(place == float(a), frames[:, 9 + a : 10 + a], total)
    return jnp.where(lane < 3.0 * H * PQ, total, 0.0)


def feature_heads():
    lane = iota((1, FEATURES), 1)
    heads = whole_part(lane, C)
    points = whole_part(lane - 256.0, 3 * PQ)
    scalars = whole_part(lane - 512.0, C)
    globals_ = whole_part(lane - 704.0, 3 * PV)
    none = jnp.full((1, FEATURES), 99.0, F32)
    heads = jnp.where(lane < 192.0, heads, none)
    heads = jnp.where((lane >= 256.0) & (lane < 400.0), points, heads)
    heads = jnp.where((lane >= 512.0) & (lane < 704.0), scalars, heads)
    return jnp.where((lane >= 704.0) & (lane < 992.0), globals_, heads)


def head_mask():
    row = whole_part(iota((LANES, FEATURES), 0), ROWS)
    return jnp.where(row == feature_heads(), 1.0, 0.0)


def fill_placing(placing):
    lane = iota((LANES, 1), 0)
    for r in range(8):
        place = jnp.full((LANES, 1), -1.0, F32)
        for first, width, base in ((0, 24, 0), (24, 18, 256), (42, 24, 512), (66, 36, 704)):
            inside = (lane >= float(first)) & (lane < float(first + width))
            place = jnp.where(inside, lane + float(base + r * width - first), place)
        at = iota((LANES, FEATURES), 1)
        placing[r * LANES : (r + 1) * LANES, :] = jnp.where(at == place, 1.0, 0.0).astype(BF16)


def per_head(values, heads):
    total = jnp.zeros(heads.shape, F32)
    for h in range(H):
        total = jnp.where(heads == float(h), values[h], total)
    return total


def softplus_of(x):
    return jnp.log(1.0 + jnp.exp(x))


def lane_heads():
    return whole_part(iota((1, LANES), 1), ROWS)


def fill_weight(expanded, bias_weight):
    row = whole_part(iota((LANES, H), 0), ROWS)
    pick = jnp.where(row == iota((LANES, H), 1), 1.0, 0.0).astype(BF16)
    rows = nt(pick, bias_weight)
    residue = iota((LANES, LANES), 0)
    residue = residue - ROWS * whole_part(residue, ROWS)
    for i in range(ROWS):
        expanded[:, i * LANES : (i + 1) * LANES] = jnp.where(
            residue == float(i), rows, 0.0
        ).astype(BF16)


def residue_masks():
    row = iota((H * ROWS, LANES), 0)
    row = row - ROWS * whole_part(row, ROWS)
    return [jnp.where(row == float(i), 1.0, 0.0).astype(BF16) for i in range(ROWS)]


def expanded_pairs(block, masks):
    pairs = block[0 : H * ROWS, :]
    wide = jnp.concatenate([pairs * m for m in masks], axis=1)
    return jnp.concatenate([wide, jnp.zeros((LANES - H * ROWS, FEATURES), BF16)], axis=0)


def expanded_features(features, mask):
    twice = jnp.concatenate([features, features], axis=0).astype(BF16)
    return jnp.concatenate([twice] * ROWS, axis=0) * mask


def wide_features(block):
    tall = block[H * ROWS :, :].astype(F32)
    return jnp.concatenate([tall[t * ROWS : (t + 1) * ROWS] for t in range(ROWS)], axis=1)


def place():
    row, col = lax.axis_index("row"), lax.axis_index("col")
    return row, col, col // 4, col % 4


def make_block(block, queries, qpoints, frames, gscalar, gpair, gpoints, wide, loss):
    f = frames[...]
    q = padded(wide, queries[...], 256)
    points = padded(wide, qpoints[...], 256)
    qg = rotated(f, points, 256, False) + shifted(f, 256)
    gs = padded(wide, gscalar[...], 256) * loss
    gg = rotated(f, padded(wide, gpoints[...], 384) * loss, 384, False)
    gg = pltpu.roll(gg, 64, 1)
    tiles = [q[:, :128], q[:, 128:], qg[:, :128], qg[:, 128:], gs[:, :128]]
    tiles += [gs[:, 128:] + gg[:, :128], gg[:, 128:256], gg[:, 256:]]
    pairs = gpair[...].astype(F32) * loss
    tall = [pairs[:, h * CZ : (h + 1) * CZ] for h in range(H)]
    block[...] = jnp.concatenate(tall + tiles, axis=0).astype(BF16)


def make_key_piece(piece, keyset, kpoints, values, vpoints, wide):
    total = padded(wide, keyset[...], 128)
    total = total + pltpu.roll(padded(wide, kpoints[...], 128), 24, 1)
    total = total + pltpu.roll(padded(wide, values[...], 128), 42, 1)
    total = total + pltpu.roll(padded(wide, vpoints[...], 128), 66, 1)
    piece[...] = total.astype(BF16)


def gather_kernel(
    loss,
    queries,
    qpoints,
    frames,
    gscalar,
    gpair,
    gpoints,
    keyset,
    kpoints,
    values,
    vpoints,
    blocks,
    pieces,
    own_block,
    own_piece,
    wide,
    send_sem,
    recv_sem,
    key_send,
    key_recv,
    own_sem,
):
    row, col, z, y = place()
    barrier = pltpu.get_barrier_semaphore()
    for d in (1, 2, 3):
        pl.semaphore_signal(
            barrier, 1, device_id=(row, z * 4 + (y + d) % 4), device_id_type=MESH
        )
    for d in (1, 7):
        pl.semaphore_signal(
            barrier, 1, device_id=(row, ((z + d) % 8) * 4 + y), device_id_type=MESH
        )
    for d in range(1, 8):
        pl.semaphore_signal(barrier, 1, device_id=((row + d) % 8, col), device_id_type=MESH)
    make_block(own_block, queries, qpoints, frames, gscalar, gpair, gpoints, wide, loss)
    make_key_piece(own_piece, keyset, kpoints, values, vpoints, wide)
    pl.semaphore_wait(barrier, 12)
    own_copy = pltpu.make_async_copy(own_block, blocks.at[col], own_sem.at[0])
    own_copy.start()
    key_copy = pltpu.make_async_copy(own_piece, pieces.at[row], own_sem.at[1])
    key_copy.start()
    sends = []

    def send(source, slot, target, at):
        copy = pltpu.make_async_remote_copy(
            source, blocks.at[slot], send_sem.at[at], recv_sem.at[slot], target, MESH
        )
        copy.start()
        sends.append(copy)

    def arrived(slot):
        pltpu.make_async_remote_copy(
            own_block, blocks.at[slot], send_sem.at[0], recv_sem.at[slot], (row, col), MESH
        ).wait_recv()

    up = (row, ((z + 1) % 8) * 4 + y)
    down = (row, ((z + 7) % 8) * 4 + y)
    at = 0
    send(own_block, col, up, 0)
    send(own_block, col, down, 1)
    at = 2
    for d in (1, 3, 2):
        send(own_block, col, (row, z * 4 + (y + d) % 4), at)
        at += 1
    key_sends = []
    for d in range(1, 8):
        copy = pltpu.make_async_remote_copy(
            own_piece,
            pieces.at[row],
            key_send.at[d],
            key_recv.at[row],
            ((row + d) % 8, col),
            MESH,
        )
        copy.start()
        key_sends.append(copy)
    for d in (1, 3, 2):
        slot = z * 4 + (y + d) % 4
        arrived(slot)
        send(blocks.at[slot], slot, up, at)
        send(blocks.at[slot], slot, down, at + 1)
        at += 2
    for s in (1, 2, 3):
        for d in (0, 1, 3, 2):
            low = ((z + 8 - s) % 8) * 4 + (y + d) % 4
            arrived(low)
            if s < 3 or d in (0, 1):
                send(blocks.at[low], low, up, at)
                at += 1
            high = ((z + s) % 8) * 4 + (y + d) % 4
            arrived(high)
            if s < 3 or d in (3, 2):
                send(blocks.at[high], high, down, at)
                at += 1
    far = ((z + 4) % 8) * 4
    for d in (0, 1, 3, 2):
        arrived(far + (y + d) % 4)
    for d in range(1, 8):
        source = (row + d) % 8
        pltpu.make_async_remote_copy(
            own_piece, pieces.at[source], key_send.at[d], key_recv.at[source], (row, col), MESH
        ).wait_recv()
    for copy in sends + key_sends:
        copy.wait_send()
    own_copy.wait()
    key_copy.wait()


def forward_setup(pieces, weight, mask, expanded, placing, keys, square, mask_ref):
    mask[...] = head_mask().astype(BF16)
    fill_placing(placing)
    fill_weight(expanded, weight[...])
    tall = jnp.concatenate([pieces[r] for r in range(8)], axis=1)
    keys[...] = nn(tall, placing[...]).astype(BF16)
    points = keys[:, 256:512].astype(F32)
    squares = points * points
    high = squares.astype(BF16)
    low = (squares - high.astype(F32)).astype(BF16)
    pick = mask[:, 256:512]
    square[...] = nt(high, pick) + nt(low, pick)


def forward_group(pairs, block, masks, mask, expanded, keys, square, masking, gamma):
    features = wide_features(block)
    wide = expanded_features(features, mask[...])
    pair_side = jnp.concatenate([expanded[...], expanded_pairs(block, masks)], axis=0)
    both = nt(pairs, pair_side)
    bias, pair_part = both[:, :LANES], both[:, LANES:]
    dots = nt(keys[:, 0:256], wide[:, 0:256])
    cross = nt(keys[:, 256:512], wide[:, 256:512])
    grads = nt(keys[:, 512:1024], wide[:, 512:1024]) + pair_part
    points = features[:, 256:512]
    squares = points * points
    high = squares.astype(BF16).astype(F32)
    pick = mask[:, 256:512]
    parts = jnp.concatenate(
        [expanded_features(high, pick), expanded_features(squares - high, pick)], axis=1
    )
    query_square = nt(jnp.ones((ROWS, 512), BF16), parts)[0:1, :]
    distance = query_square + square[...] - 2.0 * cross
    scores = WL * (dots * 0.25 + bias) - (DIST_WEIGHT * gamma) * distance - masking
    top = jnp.max(scores, axis=0, keepdims=True)
    weights = jnp.exp(scores - top)
    total = jnp.sum(weights, axis=0, keepdims=True)
    inner = jnp.sum(weights * grads, axis=0, keepdims=True)
    return weights, grads, distance, top, total, inner


def forward_kernel(
    steps,
    pair,
    blocks,
    pieces,
    weight,
    head_weight,
    key_mask,
    weights,
    grads,
    distance,
    stats,
    mask,
    expanded,
    placing,
    keys,
    square,
):
    @pl.when(pl.program_id(0) == 0)
    def _():
        forward_setup(pieces, weight, mask, expanded, placing, keys, square, None)

    masks = residue_masks()
    gamma = softplus_of(per_head(head_weight, lane_heads()))
    masking = 100000.0 * (1.0 - key_mask[...].astype(F32))
    for k in range(steps):
        pairs = jnp.concatenate([pair[k * ROWS + i] for i in range(ROWS)], axis=1)
        out = forward_group(
            pairs, blocks[k], masks, mask, expanded, keys, square, masking, gamma
        )
        weights[k], grads[k], distance[k] = out[0], out[1], out[2]
        for n in range(3):
            stats[k, :, n * LANES : (n + 1) * LANES] = out[3 + n]


def exchange(source, target, send_sem, recv_sem):
    row, col = lax.axis_index("row"), lax.axis_index("col")
    copies = []
    for d in range(1, 32):
        peer = (col + d) % 32
        copy = pltpu.make_async_remote_copy(
            source.at[peer], target.at[col], send_sem.at[d], recv_sem.at[col], (row, peer), MESH
        )
        copy.start()
        copies.append(copy)
    target[col] = source[col]
    for d in range(1, 32):
        peer = (col + d) % 32
        pltpu.make_async_remote_copy(
            source.at[peer], target.at[peer], send_sem.at[d], recv_sem.at[peer], (row, peer), MESH
        ).wait_recv()
    return copies


def combine_stats(arrived, answers, table):
    for d in range(32):
        for n in range(3):
            table[n, d : d + 1, :] = arrived[d, :, n * LANES : (n + 1) * LANES]
    tops = table[0]
    top = jnp.max(tops, axis=0, keepdims=True)
    factors = jnp.exp(tops - top)
    total = jnp.sum(factors * table[1], axis=0, keepdims=True)
    inner = jnp.sum(factors * table[2], axis=0, keepdims=True) / total
    factors = factors / total
    for d in range(32):
        answers[d, :, 0:LANES] = factors[d : d + 1, :]
        answers[d, :, LANES : 2 * LANES] = inner


def stats_kernel(stats, out, arrived, answers, table, send_a, recv_a, send_b, recv_b):
    row, col = lax.axis_index("row"), lax.axis_index("col")
    barrier = pltpu.get_barrier_semaphore()
    for d in range(1, 32):
        pl.semaphore_signal(barrier, 1, device_id=(row, (col + d) % 32), device_id_type=MESH)
    pl.semaphore_wait(barrier, 31)
    first = exchange(stats, arrived, send_a, recv_a)
    combine_stats(arrived, answers, table)
    second = exchange(answers, out, send_b, recv_b)
    for copy in first + second:
        copy.wait_send()


def backward_group(
    pairs, block, masks, factor, inner, weights, grads, distance, mask, head_rows, expanded, keys,
    point_gamma, flipped,
):
    probs = weights * factor
    score = probs * (grads - inner)
    head_part = jnp.sum(score * distance, axis=0, keepdims=True)
    scaled = WL * score
    score_half, probs_half = scaled.astype(BF16), probs.astype(BF16)
    pair_side = jnp.concatenate([expanded[...], expanded_pairs(block, masks)], axis=0)
    pair_grad = nn(jnp.concatenate([score_half, probs_half], axis=1), pair_side)
    features = wide_features(block)
    wide = expanded_features(features, mask[...])
    key_part = jnp.concatenate(
        [nn(score_half, wide[:, 0:512]), nn(probs_half, wide[:, 512:1024])], axis=1
    )
    key_sum = nn(score_half, mask[:, 256:512])
    turned = score_half.astype(F32).T
    flipped[...] = turned
    bias_part = jnp.zeros((16, LANES), F32)
    for i in range(ROWS):
        rows = flipped[pl.ds(i, 16, stride=ROWS), :].astype(BF16)
        bias_part = bias_part + nn(rows, pairs[i])
    product = nn(turned.astype(BF16), keys[:, 0:512])
    row_sum = jnp.sum(turned, axis=1, keepdims=True)
    query_part = jnp.zeros((ROWS, 512), F32)
    row_part = jnp.zeros((ROWS, 256), F32)
    for h in range(H):
        at = slice(h * ROWS, (h + 1) * ROWS)
        query_part = query_part + head_rows[at, :] * product[at, :]
        row_part = row_part + head_rows[at, 256:512] * row_sum[at, :]
    vectors = 0.25 * query_part[:, 0:256]
    points = (WC * point_gamma) * (query_part[:, 256:512] - features[:, 256:512] * row_part)
    points = pltpu.roll(points, 64, 1)
    query_out = jnp.concatenate(
        [vectors[:, :128], vectors[:, 128:] + points[:, :128], points[:, 128:]], axis=1
    )
    return pair_grad, key_part, key_sum, bias_part, head_part, query_out


def backward_kernel(
    steps,
    pair,
    blocks,
    answers,
    weights,
    grads,
    distance,
    pieces,
    weight,
    head_weight,
    pair_grad,
    query_parts,
    key_parts,
    totals,
    mask,
    head_rows,
    expanded,
    placing,
    keys,
    key_acc,
    sum_acc,
    bias_acc,
    head_acc,
    flipped,
):
    @pl.when(pl.program_id(0) == 0)
    def _():
        full = head_mask()
        mask[...] = full.astype(BF16)
        head_rows[...] = full[0 : H * ROWS, 0:512]
        fill_placing(placing)
        fill_weight(expanded, weight[...])
        tall = jnp.concatenate([pieces[r] for r in range(8)], axis=1)
        keys[...] = nn(tall, placing[...]).astype(BF16)
        key_acc[...] = jnp.zeros_like(key_acc)
        sum_acc[...] = jnp.zeros_like(sum_acc)
        bias_acc[...] = jnp.zeros_like(bias_acc)
        head_acc[...] = jnp.zeros_like(head_acc)

    masks = residue_masks()
    heads = feature_heads()[:, 256:512]
    point_gamma = softplus_of(per_head(head_weight, heads))
    key_total, sum_total = key_acc[...], sum_acc[...]
    bias_total, head_total = bias_acc[...], head_acc[...]
    for k in range(steps):
        pairs = [pair[k * ROWS + i] for i in range(ROWS)]
        out = backward_group(
            pairs,
            blocks[k],
            masks,
            answers[k, :, 0:LANES],
            answers[k, :, LANES : 2 * LANES],
            weights[k],
            grads[k],
            distance[k],
            mask,
            head_rows,
            expanded,
            keys,
            point_gamma,
            flipped,
        )
        for i in range(ROWS):
            pair_grad[k * ROWS + i] = out[0][:, i * LANES : (i + 1) * LANES].astype(BF16)
        key_total = key_total + out[1]
        sum_total = sum_total + out[2]
        bias_total = bias_total + out[3]
        head_total = head_total + out[4]
        query_parts[k] = out[5].astype(BF16)
    key_acc[...], sum_acc[...] = key_total, sum_total
    bias_acc[...], head_acc[...] = bias_total, head_total

    @pl.when(pl.program_id(0) == pl.num_programs(0) - 1)
    def _():
        points = (WC * point_gamma) * (
            key_total[:, 256:512] - keys[:, 256:512].astype(F32) * sum_total
        )
        whole = jnp.concatenate(
            [0.25 * key_total[:, 0:256], points, key_total[:, 512:1024]], axis=1
        ).astype(BF16)
        spread = nt(whole, placing[...])
        for r in range(8):
            key_parts[r] = spread[:, r * LANES : (r + 1) * LANES].astype(BF16)
        totals[0:16, :] = bias_total
        totals[16:24, :] = jnp.broadcast_to(head_total, (ROWS, LANES))


def reduce_kernel(
    residues,
    query_parts,
    key_parts,
    totals,
    frames,
    head_weight,
    queries_grad,
    qpoints_grad,
    keyset_grad,
    kpoints_grad,
    values_grad,
    vpoints_grad,
    bias_grad,
    head_grad,
    query_in,
    key_in,
    row_in,
    y_in,
    z_in,
    held,
    query_send,
    query_recv,
    key_send,
    key_recv,
    total_send,
    total_recv,
):
    row, col, z, y = place()
    barrier = pltpu.get_barrier_semaphore()
    for d in range(1, 32):
        pl.semaphore_signal(barrier, 1, device_id=(row, (col + d) % 32), device_id_type=MESH)
    for d in range(1, 8):
        pl.semaphore_signal(barrier, 1, device_id=((row + d) % 8, col), device_id_type=MESH)
    pl.semaphore_wait(barrier, 38)
    copies = []

    def remote(source, target, send, recv, device):
        return pltpu.make_async_remote_copy(source, target, send, recv, device, MESH)

    def spread(source, target, me, count, base, device):
        for d in range(1, count):
            copy = remote(
                source,
                target.at[me],
                total_send.at[base + d],
                total_recv.at[base + me],
                device((me + d) % count),
            )
            copy.start()
            copies.append(copy)

    def collect(source, target, me, count, base):
        for d in range(1, count):
            peer = (me + d) % count
            remote(
                source, target.at[peer], total_send.at[base + d], total_recv.at[base + peer], (row, col)
            ).wait_recv()

    spread(totals, row_in, row, 8, 0, lambda p: (p, col))
    for d in range(1, 8):
        peer = (row + d) % 8
        copy = remote(
            key_parts.at[peer], key_in.at[row], key_send.at[d], key_recv.at[row], (peer, col)
        )
        copy.start()
        copies.append(copy)
    for d in range(1, 32):
        peer = (col + d) % 32
        copy = remote(
            query_parts.at[peer], query_in.at[col], query_send.at[d], query_recv.at[col], (row, peer)
        )
        copy.start()
        copies.append(copy)
    row_in[row] = totals[...]
    collect(totals, row_in, row, 8, 0)
    held[0] = sum_of(row_in, 8)
    spread(held.at[0], y_in, y, 4, 8, lambda p: (row, z * 4 + p))
    y_in[y] = held[0]
    key_in[row] = key_parts[row]
    for d in range(1, 8):
        peer = (row + d) % 8
        remote(
            key_parts.at[peer], key_in.at[peer], key_send.at[d], key_recv.at[peer], (row, col)
        ).wait_recv()
    total = sum_of(key_in, 8)
    keyset_grad[...] = total[:, 0:24]
    kpoints_grad[...] = pltpu.roll(total, LANES - 24, 1)[:, 0:18]
    values_grad[...] = pltpu.roll(total, LANES - 42, 1)[:, 0:24]
    vpoints_grad[...] = pltpu.roll(total, LANES - 66, 1)[:, 0:36]
    collect(held.at[0], y_in, y, 4, 8)
    held[1] = sum_of(y_in, 4)
    spread(held.at[1], z_in, z, 8, 12, lambda p: (row, p * 4 + y))
    z_in[z] = held[1]
    query_in[col] = query_parts[col]
    for d in range(1, 32):
        peer = (col + d) % 32
        remote(
            query_parts.at[peer], query_in.at[peer], query_send.at[d], query_recv.at[peer], (row, col)
        ).wait_recv()
    mine = sum_of(query_in, 32)
    queries_grad[...] = mine[:, 0:192]
    points = pltpu.roll(mine, 384 - 192, 1)[:, 0:256]
    lane = iota((ROWS, 256), 1)
    points = jnp.where(lane < 3.0 * H * PQ, points, 0.0)
    qpoints_grad[...] = rotated(frames[...], points, 256, True)[:, 0 : 3 * H * PQ]
    collect(held.at[1], z_in, z, 8, 12)
    whole = sum_of(z_in, 8)
    turned = (whole[0:16, :] * (1.0 / residues)).T
    bias_grad[...] = turned[:, 0:H]
    heads = lane_heads()
    raw = per_head(head_weight, heads)
    line = whole[16:17, :] * (-DIST_WEIGHT / residues) / (1.0 + jnp.exp(-raw))
    for h in range(H):
        head_grad[h] = jnp.sum(jnp.where(heads == float(h), line, 0.0))
    for copy in copies:
        copy.wait_send()


def sum_of(ref, count):
    total = ref[0].astype(F32)
    for k in range(1, count):
        total = total + ref[k].astype(F32)
    return total


def shape(*dims, dtype=F32):
    return jax.ShapeDtypeStruct(dims, dtype)


VMEM = pl.BlockSpec(memory_space=pltpu.VMEM)
SMEM = pl.BlockSpec(memory_space=pltpu.SMEM)
DMA = pltpu.SemaphoreType.DMA
STEPS = 4


def local(
    pair_rep,
    queries,
    qpoints,
    frames,
    keyset,
    kpoints,
    values,
    vpoints,
    key_mask,
    bias_weight,
    head_weight,
    grad_scalar,
    grad_pair,
    grad_points,
):
    rows, keys, _ = pair_rep.shape
    residues = queries.shape[0] * 256
    loss = float(residues // 16)
    groups = rows // ROWS
    blocks, pieces = pl.pallas_call(
        functools.partial(gather_kernel, loss),
        out_shape=(shape(groups, 160, LANES, dtype=BF16), shape(8, keys, LANES, dtype=BF16)),
        in_specs=[VMEM] * 10,
        out_specs=(VMEM, VMEM),
        scratch_shapes=[
            pltpu.VMEM((160, LANES), BF16),
            pltpu.VMEM((keys, LANES), BF16),
            pltpu.VMEM((keys, 384), F32),
            DMA((32,)),
            DMA((32,)),
            DMA((8,)),
            DMA((8,)),
            DMA((2,)),
        ],
        compiler_params=pltpu.CompilerParams(collective_id=0, has_side_effects=True),
        name="gather",
    )(
        queries,
        qpoints,
        frames,
        grad_scalar,
        grad_pair,
        grad_points,
        keyset,
        kpoints,
        values,
        vpoints,
    )
    count = groups // STEPS
    per_step = lambda *dims: pl.BlockSpec((STEPS, *dims), lambda g: (g,) + (0,) * len(dims))
    pair_spec = pl.BlockSpec((STEPS * ROWS, keys, LANES), lambda g: (g, 0, 0))
    whole = lambda *dims: pl.BlockSpec(dims, lambda g: (0,) * len(dims))
    tables = [
        pltpu.VMEM((LANES, FEATURES), BF16),
        pltpu.VMEM((FEATURES, FEATURES), BF16),
        pltpu.VMEM((keys, FEATURES), BF16),
    ]
    mask_column = key_mask.reshape(keys, 1)
    weights, grads, distance, stats = pl.pallas_call(
        functools.partial(forward_kernel, STEPS),
        grid=(count,),
        out_shape=(
            shape(groups, keys, LANES),
            shape(groups, keys, LANES),
            shape(groups, keys, LANES),
            shape(groups, 1, 3 * LANES),
        ),
        in_specs=[
            pair_spec,
            per_step(160, LANES),
            whole(8, keys, LANES),
            whole(CZ, H),
            SMEM,
            whole(keys, 1),
        ],
        out_specs=(
            per_step(keys, LANES),
            per_step(keys, LANES),
            per_step(keys, LANES),
            per_step(1, 3 * LANES),
        ),
        scratch_shapes=[
            pltpu.VMEM((LANES, FEATURES), BF16),
            *tables,
            pltpu.VMEM((keys, LANES), F32),
        ],
        name="forward",
    )(pair_rep, blocks, pieces, bias_weight, head_weight, mask_column)
    answers = pl.pallas_call(
        stats_kernel,
        out_shape=shape(groups, 1, 2 * LANES),
        in_specs=[VMEM],
        out_specs=VMEM,
        scratch_shapes=[
            pltpu.VMEM((groups, 1, 3 * LANES), F32),
            pltpu.VMEM((groups, 1, 2 * LANES), F32),
            pltpu.VMEM((3, groups, LANES), F32),
            DMA((32,)),
            DMA((32,)),
            DMA((32,)),
            DMA((32,)),
        ],
        compiler_params=pltpu.CompilerParams(collective_id=1, has_side_effects=True),
        name="statistics",
    )(stats)
    pair_grad, query_parts, key_parts, totals = pl.pallas_call(
        functools.partial(backward_kernel, STEPS),
        grid=(count,),
        out_shape=(
            shape(rows, keys, LANES, dtype=BF16),
            shape(groups, ROWS, 384, dtype=BF16),
            shape(8, keys, LANES, dtype=BF16),
            shape(24, LANES),
        ),
        in_specs=[
            pair_spec,
            per_step(160, LANES),
            per_step(1, 2 * LANES),
            per_step(keys, LANES),
            per_step(keys, LANES),
            per_step(keys, LANES),
            whole(8, keys, LANES),
            whole(CZ, H),
            SMEM,
        ],
        out_specs=(
            pair_spec,
            per_step(ROWS, 384),
            whole(8, keys, LANES),
            whole(24, LANES),
        ),
        scratch_shapes=[
            pltpu.VMEM((LANES, FEATURES), BF16),
            pltpu.VMEM((H * ROWS, 512), F32),
            *tables,
            pltpu.VMEM((keys, FEATURES), F32),
            pltpu.VMEM((keys, 256), F32),
            pltpu.VMEM((16, LANES), F32),
            pltpu.VMEM((1, LANES), F32),
            pltpu.VMEM((LANES, keys), F32),
        ],
        name="backward",
    )(pair_rep, blocks, answers, weights, grads, distance, pieces, bias_weight, head_weight)
    small = pl.pallas_call(
        functools.partial(reduce_kernel, float(residues)),
        out_shape=(
            shape(ROWS, H * C),
            shape(ROWS, 3 * H * PQ),
            shape(keys, 24),
            shape(keys, 18),
            shape(keys, 24),
            shape(keys, 36),
            shape(CZ, H),
            shape(H),
        ),
        in_specs=[VMEM] * 4 + [SMEM],
        out_specs=(VMEM,) * 7 + (SMEM,),
        scratch_shapes=[
            pltpu.VMEM((groups, ROWS, 384), BF16),
            pltpu.VMEM((8, keys, LANES), BF16),
            pltpu.VMEM((8, 24, LANES), F32),
            pltpu.VMEM((4, 24, LANES), F32),
            pltpu.VMEM((8, 24, LANES), F32),
            pltpu.VMEM((2, 24, LANES), F32),
            DMA((32,)),
            DMA((32,)),
            DMA((8,)),
            DMA((8,)),
            DMA((20,)),
            DMA((20,)),
        ],
        compiler_params=pltpu.CompilerParams(collective_id=2, has_side_effects=True),
        name="sums",
    )(query_parts, key_parts, totals, frames, head_weight)
    return (pair_grad, *small)


def solution(mesh):
    both = ("row", "col")
    return jax.shard_map(
        local,
        mesh=mesh,
        in_specs=(
            P("row", "col", None),
            P(both, None),
            P(both, None),
            P(both, None),
            P("col", "row"),
            P("col", "row"),
            P("col", "row"),
            P("col", "row"),
            P("col"),
            P(),
            P(),
            P(both, None),
            P(both, None),
            P(both, None),
        ),
        out_specs=(
            P("row", "col", None),
            P(both, None),
            P(both, None),
            P("col", "row"),
            P("col", "row"),
            P("col", "row"),
            P("col", "row"),
            P(),
            P(),
        ),
        check_vma=False,
    )
```

```python
import functools
import math

import jax
import jax.numpy as jnp
from jax import lax
from jax.experimental import pallas as pl
from jax.experimental.pallas import tpu as pltpu
from jax.sharding import PartitionSpec as P

H = 12
C = 16
CZ = 128
PQ = 4
PV = 8
LANES = 128
ROWS = 8
FEATURES = 1024
MESH = pl.DeviceIdType.MESH
F32 = jnp.float32
BF16 = jnp.bfloat16
WL = math.sqrt(1.0 / 3.0)
WC = math.sqrt(2.0 / (9.0 * PQ))
DIST_WEIGHT = 0.5 * WL * WC


def nt(a, b):
    return lax.dot_general(a, b, (((1,), (1,)), ((), ())), preferred_element_type=F32)


def nn(a, b):
    return lax.dot_general(a, b, (((1,), (0,)), ((), ())), preferred_element_type=F32)


def iota(shape, dim):
    return lax.broadcasted_iota(jnp.int32, shape, dim).astype(F32)


def whole_part(x, divisor):
    return jnp.floor((x + 0.5) * (1.0 / divisor))


def padded(scratch, array, width):
    rows, used = array.shape
    scratch[0:rows, 0:width] = jnp.zeros((rows, width), F32)
    scratch[0:rows, 0:used] = array.astype(F32)
    return scratch[0:rows, 0:width]


def rotated(frames, points, width, back):
    lane = iota((ROWS, width), 1)
    place = lane - 3.0 * whole_part(lane, 3)
    total = jnp.zeros((ROWS, width), F32)
    for step in range(-2, 3):
        factor = jnp.zeros((ROWS, width), F32)
        for a in range(3):
            b = a + step
            if 0 <= b < 3:
                at = 3 * b + a if back else 3 * a + b
                factor = jnp.where(place == float(a), frames[:, at : at + 1], factor)
        moved = points if step == 0 else pltpu.roll(points, (-step) % width, 1)
        total = total + factor * moved
    return total


def shifted(frames, width):
    lane = iota((ROWS, width), 1)
    place = lane - 3.0 * whole_part(lane, 3)
    total = jnp.zeros((ROWS, width), F32)
    for a in range(3):
        total = jnp.where(place == float(a), frames[:, 9 + a : 10 + a], total)
    return jnp.where(lane < 3.0 * H * PQ, total, 0.0)


def feature_heads():
    lane = iota((1, FEATURES), 1)
    heads = whole_part(lane, C)
    points = whole_part(lane - 256.0, 3 * PQ)
    scalars = whole_part(lane - 512.0, C)
    globals_ = whole_part(lane - 704.0, 3 * PV)
    none = jnp.full((1, FEATURES), 99.0, F32)
    heads = jnp.where(lane < 192.0, heads, none)
    heads = jnp.where((lane >= 256.0) & (lane < 400.0), points, heads)
    heads = jnp.where((lane >= 512.0) & (lane < 704.0), scalars, heads)
    return jnp.where((lane >= 704.0) & (lane < 992.0), globals_, heads)


def head_mask():
    row = whole_part(iota((LANES, FEATURES), 0), ROWS)
    return jnp.where(row == feature_heads(), 1.0, 0.0)


def fill_placing(placing):
    lane = iota((LANES, 1), 0)
    for r in range(8):
        place = jnp.full((LANES, 1), -1.0, F32)
        for first, width, base in ((0, 24, 0), (24, 18, 256), (42, 24, 512), (66, 36, 704)):
            inside = (lane >= float(first)) & (lane < float(first + width))
            place = jnp.where(inside, lane + float(base + r * width - first), place)
        at = iota((LANES, FEATURES), 1)
        placing[r * LANES : (r + 1) * LANES, :] = jnp.where(at == place, 1.0, 0.0).astype(BF16)


def per_head(values, heads):
    total = jnp.zeros(heads.shape, F32)
    for h in range(H):
        total = jnp.where(heads == float(h), values[h], total)
    return total


def softplus_of(x):
    return jnp.log(1.0 + jnp.exp(x))


def lane_heads():
    return whole_part(iota((1, LANES), 1), ROWS)


def fill_weight(expanded, bias_weight):
    row = whole_part(iota((LANES, H), 0), ROWS)
    pick = jnp.where(row == iota((LANES, H), 1), 1.0, 0.0).astype(BF16)
    rows = nn(pick, bias_weight)
    residue = iota((LANES, LANES), 0)
    residue = residue - ROWS * whole_part(residue, ROWS)
    for i in range(ROWS):
        expanded[:, i * LANES : (i + 1) * LANES] = jnp.where(
            residue == float(i), rows, 0.0
        ).astype(BF16)


def residue_masks():
    row = iota((H * ROWS, LANES), 0)
    row = row - ROWS * whole_part(row, ROWS)
    return [jnp.where(row == float(i), 1.0, 0.0).astype(BF16) for i in range(ROWS)]


def expanded_pairs(block, masks):
    pairs = block[0 : H * ROWS, :]
    wide = jnp.concatenate([pairs * m for m in masks], axis=1)
    return jnp.concatenate([wide, jnp.zeros((LANES - H * ROWS, FEATURES), BF16)], axis=0)


def expanded_features(features, mask):
    twice = jnp.concatenate([features, features], axis=0).astype(BF16)
    return jnp.concatenate([twice] * ROWS, axis=0) * mask


def wide_features(block):
    tall = block[H * ROWS :, :].astype(F32)
    return jnp.concatenate([tall[t * ROWS : (t + 1) * ROWS] for t in range(ROWS)], axis=1)


def make_block(block, queries, qpoints, frames, gscalar, gpair, gpoints, wide, loss):
    f = frames[...]
    q = padded(wide, queries[...], 256)
    points = padded(wide, qpoints[...], 256)
    qg = rotated(f, points, 256, False) + shifted(f, 256)
    gs = padded(wide, gscalar[...], 256) * loss
    gg = rotated(f, padded(wide, gpoints[...], 384) * loss, 384, False)
    gg = pltpu.roll(gg, 64, 1)
    tiles = [q[:, :128], q[:, 128:], qg[:, :128], qg[:, 128:], gs[:, :128]]
    tiles += [gs[:, 128:] + gg[:, :128], gg[:, 128:256], gg[:, 256:]]
    pairs = gpair[...].astype(F32) * loss
    tall = [pairs[:, h * CZ : (h + 1) * CZ] for h in range(H)]
    block[...] = jnp.concatenate(tall + tiles, axis=0).astype(BF16)


def make_key_piece(piece, keyset, kpoints, values, vpoints, tall):
    at = 0
    tall[...] = jnp.zeros_like(tall)
    for array in (keyset, kpoints, values, vpoints):
        tall[at : at + array.shape[0], :] = array[...].astype(F32)
        at += array.shape[0]
    piece[...] = tall[...].T.astype(BF16)


def gray(i):
    return i + (i // 2) * (1 - 2 * (i % 2))


def ring_slots(e, z, y):
    s, i = (e + 2) // 4, (e + 2) % 4
    turn = s // 4 + (4 - s) // 4
    low = ((z + 8 - s) % 8) * 4 + (y + gray(i)) % 4
    high = ((z + s) % 8) * 4 + (y + gray((i + 2 * turn) % 4)) % 4
    return low, high


def near_slot(n, z, y):
    m, i = n // 4, n % 4
    dz = ((m + 1) // 2) * (2 * (m % 2) - 1)
    return ((z + 8 + dz) % 8) * 4 + (y + gray(i)) % 4


def forward_group(pairs, block, masks, mask, expanded, keys, square, masking, gamma):
    features = wide_features(block)
    wide = expanded_features(features, mask[...])
    pair_side = jnp.concatenate([expanded[...], expanded_pairs(block, masks)], axis=0)
    both = nt(pairs, pair_side)
    bias, pair_part = both[:, :LANES], both[:, LANES:]
    dots = nt(keys[:, 0:256], wide[:, 0:256])
    cross = nt(keys[:, 256:512], wide[:, 256:512])
    grads = nt(keys[:, 512:1024], wide[:, 512:1024]) + pair_part
    points = features[:, 256:512]
    squares = points * points
    high = squares.astype(BF16).astype(F32)
    pick = mask[:, 256:512]
    parts = jnp.concatenate(
        [expanded_features(high, pick), expanded_features(squares - high, pick)], axis=1
    )
    query_square = nt(jnp.ones((ROWS, 512), BF16), parts)[0:1, :]
    distance = query_square + square[...] - 2.0 * cross
    scores = WL * (dots * 0.25 + bias) - (DIST_WEIGHT * gamma) * distance - masking
    top = jnp.max(scores, axis=0, keepdims=True)
    weights = jnp.exp(scores - top)
    total = jnp.sum(weights, axis=0, keepdims=True)
    inner = jnp.sum(weights * grads, axis=0, keepdims=True)
    return weights, grads, distance, top, total, inner


def combine_stats(arrived, answers, table):
    for d in range(32):
        for n in range(3):
            table[n, d : d + 1, :] = arrived[d, :, n * LANES : (n + 1) * LANES]
    tops = table[0]
    top = jnp.max(tops, axis=0, keepdims=True)
    factors = jnp.exp(tops - top)
    total = jnp.sum(factors * table[1], axis=0, keepdims=True)
    inner = jnp.sum(factors * table[2], axis=0, keepdims=True) / total
    factors = factors / total
    for d in range(32):
        answers[d, :, 0:LANES] = factors[d : d + 1, :]
        answers[d, :, LANES : 2 * LANES] = inner


def score_group(factor, inner, weights, grads, distance):
    probs = weights * factor
    score = probs * (grads - inner)
    head_part = jnp.sum(score * distance, axis=0, keepdims=True)
    return (WL * score).astype(BF16), probs.astype(BF16), head_part


def bias_group(score_half, pairs, flipped):
    turned = score_half.astype(F32).T
    flipped[...] = turned
    bias_part = jnp.zeros((16, LANES), F32)
    for i in range(ROWS):
        rows = flipped[pl.ds(i, 16, stride=ROWS), :].astype(BF16)
        bias_part = bias_part + nn(rows, pairs[i])
    return turned.astype(BF16), bias_part


def small_group(score_half, probs_half, turned, block, mask, head_rows, keys, point_gamma):
    features = wide_features(block)
    wide = expanded_features(features, mask[...])
    key_part = jnp.concatenate(
        [nn(score_half, wide[:, 0:512]), nn(probs_half, wide[:, 512:1024])], axis=1
    )
    key_sum = nn(score_half, mask[:, 256:512])
    product = nn(turned, keys[:, 0:512])
    row_sum = jnp.sum(turned.astype(F32), axis=1, keepdims=True)
    query_part = jnp.zeros((ROWS, 512), F32)
    row_part = jnp.zeros((ROWS, 256), F32)
    for h in range(H):
        at = slice(h * ROWS, (h + 1) * ROWS)
        query_part = query_part + head_rows[at, :] * product[at, :]
        row_part = row_part + head_rows[at, 256:512] * row_sum[at, :]
    vectors = 0.25 * query_part[:, 0:256]
    points = (WC * point_gamma) * (query_part[:, 256:512] - features[:, 256:512] * row_part)
    points = pltpu.roll(points, 64, 1)
    query_out = jnp.concatenate(
        [vectors[:, :128], vectors[:, 128:] + points[:, :128], points[:, 128:]], axis=1
    )
    return key_part, key_sum, query_out


def sum_of(ref, count):
    total = ref[0].astype(F32)
    for k in range(1, count):
        total = total + ref[k].astype(F32)
    return total


def main_kernel(
    loss,
    residues,
    pair_hbm,
    queries,
    qpoints,
    frames,
    keyset,
    kpoints,
    values,
    vpoints,
    key_mask,
    weight,
    head_weight,
    gscalar,
    gpair,
    gpoints,
    halves_out,
    blocks_out,
    query_out,
    key_out,
    total_out,
    pair,
    blocks,
    own_block,
    pieces,
    own_piece,
    piece_rows,
    wide,
    mask,
    head_rows,
    expanded,
    placing,
    keys,
    square,
    weights,
    grads,
    distance,
    stats,
    arrived,
    answers,
    answered,
    table,
    halves,
    turned,
    flipped,
    key_acc,
    sum_acc,
    bias_acc,
    head_acc,
    query_parts,
    query_in,
    key_parts,
    key_in,
    totals,
    row_in,
    y_in,
    z_in,
    pair_sem,
    own_sem,
    out_sem,
    send_sem,
    recv_sem,
    key_send,
    key_recv,
    stats_send,
    stats_recv,
    answer_send,
    answer_recv,
    query_send,
    query_recv,
    part_send,
    part_recv,
    total_send,
    total_recv,
):
    row, col = lax.axis_index("row"), lax.axis_index("col")
    z, y = col // 4, col % 4
    here = (row, col)
    groups = blocks.shape[0]

    def remote(source, target, send, recv, device):
        return pltpu.make_async_remote_copy(source, target, send, recv, device, MESH)

    barrier = pltpu.get_barrier_semaphore()
    for d in range(1, 32):
        pl.semaphore_signal(barrier, 1, device_id=(row, (col + d) % 32), device_id_type=MESH)
    for d in range(1, 8):
        pl.semaphore_signal(barrier, 1, device_id=((row + d) % 8, col), device_id_type=MESH)
    quarter = pair.shape[0] // 4
    pair_copies = []
    for k in range(4):
        at = pl.ds(k * quarter, quarter)
        copy = pltpu.make_async_copy(pair_hbm.at[at], pair.at[at], pair_sem.at[k])
        copy.start()
        pair_copies.append(copy)
    make_block(own_block, queries, qpoints, frames, gscalar, gpair, gpoints, wide, loss)
    make_key_piece(own_piece, keyset, kpoints, values, vpoints, piece_rows)
    pl.semaphore_wait(barrier, 38)

    up = (row, ((z + 1) % 8) * 4 + y)
    down = (row, ((z + 7) % 8) * 4 + y)

    def send_block(source, slot, target, at):
        remote(source, blocks.at[slot], send_sem.at[at], recv_sem.at[slot], target).start()

    def block_arrived(slot):
        remote(own_block, blocks.at[slot], send_sem.at[0], recv_sem.at[slot], here).wait_recv()

    send_block(own_block, col, up, 0)
    send_block(own_block, col, down, 1)
    for n, d in enumerate((1, 3, 2)):
        send_block(own_block, col, (row, z * 4 + (y + d) % 4), 2 + n)
    for d in range(1, 8):
        peer = ((row + d) % 8, col)
        remote(own_piece, pieces.at[row], key_send.at[d], key_recv.at[row], peer).start()
    own_copy = pltpu.make_async_copy(own_block, blocks.at[col], own_sem.at[0])
    own_copy.start()
    piece_copy = pltpu.make_async_copy(own_piece, pieces.at[row], own_sem.at[1])
    piece_copy.start()

    full = head_mask()
    mask[...] = full.astype(BF16)
    head_rows[...] = full[0 : H * ROWS, 0:512]
    fill_weight(expanded, weight[...])
    fill_placing(placing)
    key_acc[...] = jnp.zeros_like(key_acc)
    sum_acc[...] = jnp.zeros_like(sum_acc)
    bias_acc[...] = jnp.zeros_like(bias_acc)
    head_acc[...] = jnp.zeros_like(head_acc)
    masks = residue_masks()
    gamma = softplus_of(per_head(head_weight, lane_heads()))
    point_gamma = softplus_of(per_head(head_weight, feature_heads()[:, 256:512]))
    masking = 100000.0 * (1.0 - key_mask[...].astype(F32))
    masking = jnp.broadcast_to(masking, (ROWS, masking.shape[1])).T[:, 0:1]

    for n, d in enumerate((1, 3, 2)):
        slot = z * 4 + (y + d) % 4
        block_arrived(slot)
        send_block(blocks.at[slot], slot, up, 5 + 2 * n)
        send_block(blocks.at[slot], slot, down, 6 + 2 * n)
    for d in range(1, 8):
        source = (row + d) % 8
        remote(own_piece, pieces.at[source], key_send.at[d], key_recv.at[source], here).wait_recv()
    piece_copy.wait()
    own_copy.wait()
    tall = jnp.concatenate([pieces[r] for r in range(8)], axis=1)
    keys[...] = nn(tall, placing[...]).astype(BF16)
    points = keys[:, 256:512].astype(F32)
    squares = points * points
    high_part = squares.astype(BF16)
    low_part = (squares - high_part.astype(F32)).astype(BF16)
    square[...] = nt(high_part, mask[:, 256:512]) + nt(low_part, mask[:, 256:512])
    for copy in pair_copies:
        copy.wait()

    def send_stats(slot):
        remote(
            stats.at[slot], arrived.at[col], stats_send.at[slot], stats_recv.at[col], (row, slot)
        ).start()

    def forward_one(slot):
        first = pl.multiple_of(slot * ROWS, ROWS)
        pairs = jnp.concatenate([pair[first + i] for i in range(ROWS)], axis=1)
        out = forward_group(
            pairs, blocks[slot], masks, mask, expanded, keys, square, masking, gamma
        )
        weights[slot], grads[slot], distance[slot] = out[0], out[1], out[2]
        for n in range(3):
            stats[slot, :, n * LANES : (n + 1) * LANES] = out[3 + n]

    def forward_step(e, _):
        low, high = ring_slots(e, z, y)

        @pl.when(e >= 2)
        def _():
            block_arrived(low)

        @pl.when((e >= 2) & (e <= 11))
        def _():
            send_block(blocks.at[low], low, up, 11 + e)

        @pl.when(e >= 2)
        def _():
            block_arrived(high)

        @pl.when(((e >= 2) & (e <= 9)) | ((e >= 12) & (e <= 13)))
        def _():
            send_block(blocks.at[high], high, down, 23 + e)

        @pl.when(e >= 1)
        def _():
            send_stats(ring_slots(e - 1, z, y)[0])

        @pl.when(e >= 2)
        def _():
            send_stats(ring_slots(e - 1, z, y)[1])

        forward_one(low)
        forward_one(high)
        return 0

    lax.fori_loop(0, 16, forward_step, 0)
    blocks_copy = pltpu.make_async_copy(blocks, blocks_out, out_sem.at[0])
    blocks_copy.start()
    arrived[col] = stats[col]
    for slot in ring_slots(15, z, y):
        send_stats(slot)

    def stats_arrived(d, _):
        peer = (col + d) % 32
        remote(
            stats.at[peer], arrived.at[peer], stats_send.at[peer], stats_recv.at[peer], here
        ).wait_recv()
        return 0

    lax.fori_loop(1, 32, stats_arrived, 0)
    combine_stats(arrived, answers, table)

    def send_answer(n, _):
        peer = near_slot(32 - n, z, y)
        remote(
            answers.at[peer], answered.at[col], answer_send.at[peer], answer_recv.at[col], (row, peer)
        ).start()
        return 0

    lax.fori_loop(1, 32, send_answer, 0)
    answered[col] = answers[col]

    def score_one(slot, k):
        first = pl.multiple_of(slot * ROWS, ROWS)
        pairs = [pair[first + i] for i in range(ROWS)]
        score_half, probs_half, head_part = score_group(
            answered[slot, :, 0:LANES],
            answered[slot, :, LANES : 2 * LANES],
            weights[slot],
            grads[slot],
            distance[slot],
        )
        halves[slot, :, 0:LANES] = score_half
        halves[slot, :, LANES : 2 * LANES] = probs_half
        turned[slot], bias_part = bias_group(score_half, pairs, flipped.at[k])
        return bias_part, head_part

    def answer_arrived(slot):
        remote(
            answers.at[slot], answered.at[slot], answer_send.at[slot], answer_recv.at[slot], here
        ).wait_recv()

    def score_step(e, _):
        first, second = near_slot(2 * e, z, y), near_slot(2 * e + 1, z, y)

        @pl.when(e >= 1)
        def _():
            answer_arrived(first)

        answer_arrived(second)
        bias_a, head_a = score_one(first, 0)
        bias_b, head_b = score_one(second, 1)
        bias_acc[...] += bias_a + bias_b
        head_acc[...] += head_a + head_b
        return 0

    lax.fori_loop(0, 16, score_step, 0)
    halves_copy = pltpu.make_async_copy(halves, halves_out, out_sem.at[1])
    halves_copy.start()
    totals[0, 0:16, :] = bias_acc[...]
    totals[0, 16:24, :] = jnp.broadcast_to(head_acc[...], (ROWS, LANES))

    def spread_total(source, target, me, count, base, device):
        for d in range(1, count):
            remote(
                source,
                target.at[me],
                total_send.at[base + d],
                total_recv.at[base + me],
                device((me + d) % count),
            ).start()

    def total_arrived(source, target, me, count, base):
        for d in range(1, count):
            peer = (me + d) % count
            remote(
                source, target.at[peer], total_send.at[base + d], total_recv.at[base + peer], here
            ).wait_recv()

    spread_total(totals.at[0], row_in, row, 8, 0, lambda p: (p, col))
    row_in[row] = totals[0]

    def send_query(slot):
        remote(
            query_parts.at[slot], query_in.at[col], query_send.at[slot], query_recv.at[col], (row, slot)
        ).start()

    def small_one(slot):
        out = small_group(
            halves[slot, :, 0:LANES],
            halves[slot, :, LANES : 2 * LANES],
            turned[slot],
            blocks[slot],
            mask,
            head_rows,
            keys,
            point_gamma,
        )
        query_parts[slot] = out[2].astype(BF16)
        return out[0], out[1]

    def small_step(e, _):
        first, second = near_slot(31 - 2 * e, z, y), near_slot(30 - 2 * e, z, y)

        @pl.when(e >= 1)
        def _():
            send_query(near_slot(33 - 2 * e, z, y))
            send_query(near_slot(32 - 2 * e, z, y))

        key_a, sum_a = small_one(first)
        key_b, sum_b = small_one(second)
        key_acc[...] += key_a + key_b
        sum_acc[...] += sum_a + sum_b
        return 0

    lax.fori_loop(0, 8, small_step, 0)
    total_arrived(totals.at[0], row_in, row, 8, 0)
    totals[1] = sum_of(row_in, 8)
    y_in[y] = totals[1]
    spread_total(totals.at[1], y_in, y, 4, 8, lambda p: (row, z * 4 + p))
    lax.fori_loop(8, 16, small_step, 0)
    send_query(near_slot(1, z, y))
    query_in[col] = query_parts[col]
    total_arrived(totals.at[1], y_in, y, 4, 8)
    totals[2] = sum_of(y_in, 4)
    z_in[z] = totals[2]
    spread_total(totals.at[2], z_in, z, 8, 12, lambda p: (row, p * 4 + y))
    key_points = (WC * point_gamma) * (
        key_acc[:, 256:512] - keys[:, 256:512].astype(F32) * sum_acc[...]
    )
    whole = jnp.concatenate(
        [0.25 * key_acc[:, 0:256], key_points, key_acc[:, 512:1024]], axis=1
    ).astype(BF16)
    spread = nt(whole, placing[...])
    for r in range(8):
        key_parts[r] = spread[:, r * LANES : (r + 1) * LANES].astype(BF16)
    key_in[row] = key_parts[row]
    for d in range(1, 8):
        peer = (row + d) % 8
        remote(
            key_parts.at[peer], key_in.at[row], part_send.at[d], part_recv.at[row], (peer, col)
        ).start()

    def query_arrived(d, _):
        peer = (col + d) % 32
        remote(
            query_parts.at[peer], query_in.at[peer], query_send.at[peer], query_recv.at[peer], here
        ).wait_recv()
        return 0

    lax.fori_loop(1, 32, query_arrived, 0)
    mine = sum_of(query_in, 32)
    query_out[:, 0:256] = mine[:, 0:256]
    back = pltpu.roll(mine, 384 - 192, 1)[:, 0:256]
    lane = iota((ROWS, 256), 1)
    back = jnp.where(lane < 3.0 * H * PQ, back, 0.0)
    query_out[:, 256:512] = rotated(frames[...], back, 256, True)
    for d in range(1, 8):
        peer = (row + d) % 8
        remote(
            key_parts.at[peer], key_in.at[peer], part_send.at[d], part_recv.at[peer], here
        ).wait_recv()
    key_out[...] = sum_of(key_in, 8).T
    total_arrived(totals.at[2], z_in, z, 8, 12)
    total_out[...] = sum_of(z_in, 8)

    for at in list(range(11)) + list(range(13, 23)) + list(range(25, 33)) + [35, 36]:
        remote(own_block, blocks.at[0], send_sem.at[at], recv_sem.at[0], here).wait_send()
    for d in range(1, 8):
        remote(own_piece, pieces.at[0], key_send.at[d], key_recv.at[0], here).wait_send()
        remote(key_parts.at[0], key_in.at[0], part_send.at[d], part_recv.at[0], here).wait_send()

    def all_left(d, _):
        peer = (col + d) % 32
        remote(
            stats.at[peer], arrived.at[peer], stats_send.at[peer], stats_recv.at[peer], here
        ).wait_send()
        remote(
            answers.at[peer], answered.at[peer], answer_send.at[peer], answer_recv.at[peer], here
        ).wait_send()
        remote(
            query_parts.at[peer], query_in.at[peer], query_send.at[peer], query_recv.at[peer], here
        ).wait_send()
        return 0

    lax.fori_loop(1, 32, all_left, 0)
    for base, count in ((0, 8), (8, 4), (12, 8)):
        for d in range(1, count):
            remote(
                totals.at[0], row_in.at[0], total_send.at[base + d], total_recv.at[0], here
            ).wait_send()
    blocks_copy.wait()
    halves_copy.wait()


def last_kernel(
    steps,
    residues,
    halves,
    blocks,
    weight,
    head_weight,
    query_sum,
    key_sum,
    total_sum,
    pair_grad,
    queries_grad,
    qpoints_grad,
    keyset_grad,
    kpoints_grad,
    values_grad,
    vpoints_grad,
    bias_grad,
    head_grad,
    expanded,
):
    @pl.when(pl.program_id(0) == 0)
    def _():
        fill_weight(expanded, weight[...])
        queries_grad[...] = query_sum[:, 0:192]
        qpoints_grad[...] = query_sum[:, 256:400]
        at = 0
        for out in (keyset_grad, kpoints_grad, values_grad, vpoints_grad):
            out[...] = key_sum[at : at + out.shape[0], :]
            at += out.shape[0]
        bias_grad[...] = total_sum[0:H, :] * (1.0 / residues)
        heads = lane_heads()
        raw = per_head(head_weight, heads)
        line = total_sum[16:17, :] * (-DIST_WEIGHT / residues) / (1.0 + jnp.exp(-raw))
        for h in range(H):
            head_grad[h] = jnp.sum(jnp.where(heads == float(h), line, 0.0))

    masks = residue_masks()
    for k in range(steps):
        pair_side = jnp.concatenate([expanded[...], expanded_pairs(blocks[k], masks)], axis=0)
        out = nn(halves[k], pair_side)
        for i in range(ROWS):
            pair_grad[k * ROWS + i] = out[:, i * LANES : (i + 1) * LANES].astype(BF16)


def shape(*dims, dtype=F32):
    return jax.ShapeDtypeStruct(dims, dtype)


VMEM = pl.BlockSpec(memory_space=pltpu.VMEM)
SMEM = pl.BlockSpec(memory_space=pltpu.SMEM)
ANY = pl.BlockSpec(memory_space=pl.ANY)
DMA = pltpu.SemaphoreType.DMA
STEPS = 4


def local(
    pair_rep,
    queries,
    qpoints,
    frames,
    keyset,
    kpoints,
    values,
    vpoints,
    key_mask,
    bias_weight,
    head_weight,
    grad_scalar,
    grad_pair,
    grad_points,
):
    rows, keys, _ = pair_rep.shape
    residues = queries.shape[0] * 256
    loss = float(residues // 16)
    groups = rows // ROWS
    weight = bias_weight.T
    full, half = pltpu.VMEM, lambda *dims: pltpu.VMEM(dims, BF16)
    halves, blocks, query_sum, key_sum, total_sum = pl.pallas_call(
        functools.partial(main_kernel, loss, float(residues)),
        out_shape=(
            shape(groups, keys, 2 * LANES, dtype=BF16),
            shape(groups, 160, LANES, dtype=BF16),
            shape(ROWS, 512),
            shape(LANES, keys),
            shape(24, LANES),
        ),
        in_specs=[ANY] + [VMEM] * 9 + [SMEM] + [VMEM] * 3,
        out_specs=(ANY, ANY, VMEM, VMEM, VMEM),
        scratch_shapes=[
            half(rows, keys, LANES),
            half(groups, 160, LANES),
            half(160, LANES),
            half(8, keys, LANES),
            half(keys, LANES),
            full((LANES, keys), F32),
            full((ROWS, 384), F32),
            half(LANES, FEATURES),
            full((H * ROWS, 512), F32),
            half(LANES, FEATURES),
            half(FEATURES, FEATURES),
            half(keys, FEATURES),
            full((keys, LANES), F32),
            full((groups, keys, LANES), F32),
            full((groups, keys, LANES), F32),
            full((groups, keys, LANES), F32),
            full((groups, 1, 3 * LANES), F32),
            full((groups, 1, 3 * LANES), F32),
            full((groups, 1, 2 * LANES), F32),
            full((groups, 1, 2 * LANES), F32),
            full((3, groups, LANES), F32),
            half(groups, keys, 2 * LANES),
            half(groups, LANES, keys),
            full((2, LANES, keys), F32),
            full((keys, FEATURES), F32),
            full((keys, 256), F32),
            full((16, LANES), F32),
            full((1, LANES), F32),
            half(groups, ROWS, 384),
            half(groups, ROWS, 384),
            half(8, keys, LANES),
            half(8, keys, LANES),
            full((3, 24, LANES), F32),
            full((8, 24, LANES), F32),
            full((4, 24, LANES), F32),
            full((8, 24, LANES), F32),
            DMA((4,)),
            DMA((2,)),
            DMA((2,)),
            DMA((40,)),
            DMA((32,)),
            DMA((8,)),
            DMA((8,)),
            DMA((32,)),
            DMA((32,)),
            DMA((32,)),
            DMA((32,)),
            DMA((32,)),
            DMA((32,)),
            DMA((8,)),
            DMA((8,)),
            DMA((20,)),
            DMA((20,)),
        ],
        compiler_params=pltpu.CompilerParams(
            collective_id=0, has_side_effects=True, vmem_limit_bytes=40 << 20
        ),
        name="main",
    )(
        pair_rep,
        queries,
        qpoints,
        frames,
        keyset.T,
        kpoints.T,
        values.T,
        vpoints.T,
        key_mask.reshape(1, keys),
        weight,
        head_weight,
        grad_scalar,
        grad_pair,
        grad_points,
    )
    per_step = lambda *dims: pl.BlockSpec((STEPS, *dims), lambda g: (g,) + (0,) * len(dims))
    whole = lambda *dims: pl.BlockSpec(dims, lambda g: (0,) * len(dims))
    finals = (
        (ROWS, H * C),
        (ROWS, 3 * H * PQ),
        (24, keys),
        (18, keys),
        (24, keys),
        (36, keys),
        (H, CZ),
    )
    pair_grad, queries_grad, qpoints_grad, *turned, bias_grad, head_grad = pl.pallas_call(
        functools.partial(last_kernel, STEPS, float(residues)),
        grid=(groups // STEPS,),
        out_shape=(
            shape(rows, keys, LANES, dtype=BF16),
            *(shape(*dims) for dims in finals),
            shape(H),
        ),
        in_specs=[
            per_step(keys, 2 * LANES),
            per_step(160, LANES),
            whole(H, CZ),
            SMEM,
            whole(ROWS, 512),
            whole(LANES, keys),
            whole(24, LANES),
        ],
        out_specs=(
            pl.BlockSpec((STEPS * ROWS, keys, LANES), lambda g: (g, 0, 0)),
            *(whole(*dims) for dims in finals),
            SMEM,
        ),
        scratch_shapes=[half(LANES, FEATURES)],
        name="last",
    )(halves, blocks, weight, head_weight, query_sum, key_sum, total_sum)
    return (
        pair_grad,
        queries_grad,
        qpoints_grad,
        *(array.T for array in turned),
        bias_grad.T,
        head_grad,
    )


def solution(mesh):
    both = ("row", "col")
    return jax.shard_map(
        local,
        mesh=mesh,
        in_specs=(
            P("row", "col", None),
            P(both, None),
            P(both, None),
            P(both, None),
            P("col", "row"),
            P("col", "row"),
            P("col", "row"),
            P("col", "row"),
            P("col"),
            P(),
            P(),
            P(both, None),
            P(both, None),
            P(both, None),
        ),
        out_specs=(
            P("row", "col", None),
            P(both, None),
            P(both, None),
            P("col", "row"),
            P("col", "row"),
            P("col", "row"),
            P("col", "row"),
            P(),
            P(),
        ),
        check_vma=False,
    )
```

```python
import functools
import math

import jax
import jax.numpy as jnp
from jax import lax
from jax.experimental import pallas as pl
from jax.experimental.pallas import tpu as pltpu
from jax.sharding import PartitionSpec as P

H = 12
C = 16
CZ = 128
PQ = 4
PV = 8
LANES = 128
ROWS = 8
FEATURES = 1024
MESH = pl.DeviceIdType.MESH
F32 = jnp.float32
BF16 = jnp.bfloat16
WL = math.sqrt(1.0 / 3.0)
WC = math.sqrt(2.0 / (9.0 * PQ))
DIST_WEIGHT = 0.5 * WL * WC


def nt(a, b):
    return lax.dot_general(a, b, (((1,), (1,)), ((), ())), preferred_element_type=F32)


def nn(a, b):
    return lax.dot_general(a, b, (((1,), (0,)), ((), ())), preferred_element_type=F32)


def iota(shape, dim):
    return lax.broadcasted_iota(jnp.int32, shape, dim).astype(F32)


def whole_part(x, divisor):
    return jnp.floor((x + 0.5) * (1.0 / divisor))


def padded(scratch, array, width):
    rows, used = array.shape
    scratch[0:rows, 0:width] = jnp.zeros((rows, width), F32)
    scratch[0:rows, 0:used] = array.astype(F32)
    return scratch[0:rows, 0:width]


def rotated(frames, points, width, back):
    lane = iota((ROWS, width), 1)
    place = lane - 3.0 * whole_part(lane, 3)
    total = jnp.zeros((ROWS, width), F32)
    for step in range(-2, 3):
        factor = jnp.zeros((ROWS, width), F32)
        for a in range(3):
            b = a + step
            if 0 <= b < 3:
                at = 3 * b + a if back else 3 * a + b
                factor = jnp.where(place == float(a), frames[:, at : at + 1], factor)
        moved = points if step == 0 else pltpu.roll(points, (-step) % width, 1)
        total = total + factor * moved
    return total


def shifted(frames, width):
    lane = iota((ROWS, width), 1)
    place = lane - 3.0 * whole_part(lane, 3)
    total = jnp.zeros((ROWS, width), F32)
    for a in range(3):
        total = jnp.where(place == float(a), frames[:, 9 + a : 10 + a], total)
    return jnp.where(lane < 3.0 * H * PQ, total, 0.0)


def feature_heads():
    lane = iota((1, FEATURES), 1)
    heads = whole_part(lane, C)
    points = whole_part(lane - 256.0, 3 * PQ)
    scalars = whole_part(lane - 512.0, C)
    globals_ = whole_part(lane - 704.0, 3 * PV)
    none = jnp.full((1, FEATURES), 99.0, F32)
    heads = jnp.where(lane < 192.0, heads, none)
    heads = jnp.where((lane >= 256.0) & (lane < 400.0), points, heads)
    heads = jnp.where((lane >= 512.0) & (lane < 704.0), scalars, heads)
    return jnp.where((lane >= 704.0) & (lane < 992.0), globals_, heads)


def head_mask():
    row = whole_part(iota((LANES, FEATURES), 0), ROWS)
    return jnp.where(row == feature_heads(), 1.0, 0.0)


def fill_placing(placing):
    lane = iota((LANES, 1), 0)
    for r in range(8):
        place = jnp.full((LANES, 1), -1.0, F32)
        for first, width, base in ((0, 24, 0), (24, 18, 256), (42, 24, 512), (66, 36, 704)):
            inside = (lane >= float(first)) & (lane < float(first + width))
            place = jnp.where(inside, lane + float(base + r * width - first), place)
        at = iota((LANES, FEATURES), 1)
        placing[r * LANES : (r + 1) * LANES, :] = jnp.where(at == place, 1.0, 0.0).astype(BF16)


def per_head(values, heads):
    total = jnp.zeros(heads.shape, F32)
    for h in range(H):
        total = jnp.where(heads == float(h), values[:, h : h + 1], total)
    return total


def softplus_of(x):
    return jnp.log(1.0 + jnp.exp(x))


def lane_heads():
    return whole_part(iota((1, LANES), 1), ROWS)


def fill_weight(expanded, bias_weight):
    row = whole_part(iota((LANES, H), 0), ROWS)
    pick = jnp.where(row == iota((LANES, H), 1), 1.0, 0.0).astype(BF16)
    rows = nn(pick, bias_weight)
    residue = iota((LANES, LANES), 0)
    residue = residue - ROWS * whole_part(residue, ROWS)
    for i in range(ROWS):
        expanded[:, i * LANES : (i + 1) * LANES] = jnp.where(
            residue == float(i), rows, 0.0
        ).astype(BF16)


def residue_masks():
    row = iota((H * ROWS, LANES), 0)
    row = row - ROWS * whole_part(row, ROWS)
    return [jnp.where(row == float(i), 1.0, 0.0).astype(BF16) for i in range(ROWS)]


def expanded_pairs(block, masks):
    pairs = block[0 : H * ROWS, :]
    wide = jnp.concatenate([pairs * m for m in masks], axis=1)
    return jnp.concatenate([wide, jnp.zeros((LANES - H * ROWS, FEATURES), BF16)], axis=0)


def expanded_features(features, mask):
    twice = jnp.concatenate([features, features], axis=0).astype(BF16)
    return jnp.concatenate([twice] * ROWS, axis=0) * mask


def wide_features(block):
    tall = block[H * ROWS :, :].astype(F32)
    return jnp.concatenate([tall[t * ROWS : (t + 1) * ROWS] for t in range(ROWS)], axis=1)


def make_block(block, queries, qpoints, frames, gscalar, gpair, gpoints, wide, loss):
    f = frames[...]
    q = padded(wide, queries[...], 256)
    points = padded(wide, qpoints[...], 256)
    qg = rotated(f, points, 256, False) + shifted(f, 256)
    gs = padded(wide, gscalar[...], 256) * loss
    gg = rotated(f, padded(wide, gpoints[...], 384) * loss, 384, False)
    gg = pltpu.roll(gg, 64, 1)
    tiles = [q[:, :128], q[:, 128:], qg[:, :128], qg[:, 128:], gs[:, :128]]
    tiles += [gs[:, 128:] + gg[:, :128], gg[:, 128:256], gg[:, 256:]]
    pairs = gpair[...].astype(F32) * loss
    tall = [pairs[:, h * CZ : (h + 1) * CZ] for h in range(H)]
    block[...] = jnp.concatenate(tall + tiles, axis=0).astype(BF16)


def make_key_piece(piece, keyset, kpoints, values, vpoints, tall):
    at = 0
    tall[...] = jnp.zeros_like(tall)
    for array in (keyset, kpoints, values, vpoints):
        tall[at : at + array.shape[0], :] = array[...].astype(F32)
        at += array.shape[0]
    piece[...] = tall[...].T.astype(BF16)


def gray(i):
    return i + (i // 2) * (1 - 2 * (i % 2))


def ring_slots(e, z, y):
    s, i = (e + 2) // 4, (e + 2) % 4
    turn = s // 4 + (4 - s) // 4
    low = ((z + 8 - s) % 8) * 4 + (y + gray(i)) % 4
    high = ((z + s) % 8) * 4 + (y + gray((i + 2 * turn) % 4)) % 4
    return low, high


def near_slot(n, z, y):
    m, i = n // 4, n % 4
    dz = ((m + 1) // 2) * (2 * (m % 2) - 1)
    return ((z + 8 + dz) % 8) * 4 + (y + gray(i)) % 4


def forward_group(pairs, block, masks, mask, expanded, keys, square, masking, gamma):
    features = wide_features(block)
    wide = expanded_features(features, mask[...])
    pair_side = jnp.concatenate([expanded[...], expanded_pairs(block, masks)], axis=0)
    both = nt(pairs, pair_side)
    bias, pair_part = both[:, :LANES], both[:, LANES:]
    dots = nt(keys[:, 0:256], wide[:, 0:256])
    cross = nt(keys[:, 256:512], wide[:, 256:512])
    grads = nt(keys[:, 512:1024], wide[:, 512:1024]) + pair_part
    points = features[:, 256:512]
    squares = points * points
    high = squares.astype(BF16).astype(F32)
    pick = mask[:, 256:512]
    parts = jnp.concatenate(
        [expanded_features(high, pick), expanded_features(squares - high, pick)], axis=1
    )
    query_square = nt(jnp.ones((ROWS, 512), BF16), parts)[0:1, :]
    distance = query_square + square[...] - 2.0 * cross
    scores = WL * (dots * 0.25 + bias) - (DIST_WEIGHT * gamma) * distance - masking
    top = jnp.max(scores, axis=0, keepdims=True)
    weights = jnp.exp(scores - top)
    total = jnp.sum(weights, axis=0, keepdims=True)
    inner = jnp.sum(weights * grads, axis=0, keepdims=True)
    return weights, grads, distance, top, total, inner


def combine_stats(arrived, answers, table):
    for d in range(32):
        for n in range(3):
            table[n, d : d + 1, :] = arrived[d, :, n * LANES : (n + 1) * LANES]
    tops = table[0]
    top = jnp.max(tops, axis=0, keepdims=True)
    factors = jnp.exp(tops - top)
    total = jnp.sum(factors * table[1], axis=0, keepdims=True)
    inner = jnp.sum(factors * table[2], axis=0, keepdims=True) / total
    factors = factors / total
    for d in range(32):
        answers[d, :, 0:LANES] = factors[d : d + 1, :]
        answers[d, :, LANES : 2 * LANES] = inner


def score_group(factor, inner, weights, grads, distance):
    probs = weights * factor
    score = probs * (grads - inner)
    head_part = jnp.sum(score * distance, axis=0, keepdims=True)
    return (WL * score).astype(BF16), probs.astype(BF16), head_part


def bias_group(score_half, pairs, flipped):
    turned = score_half.astype(F32).T
    flipped[...] = turned
    bias_part = jnp.zeros((16, LANES), F32)
    for i in range(ROWS):
        rows = flipped[pl.ds(i, 16, stride=ROWS), :].astype(BF16)
        bias_part = bias_part + nn(rows, pairs[i])
    return turned.astype(BF16), bias_part


def small_group(score_half, probs_half, turned, block, mask, head_rows, keys, point_gamma):
    features = wide_features(block)
    wide = expanded_features(features, mask[...])
    key_part = jnp.concatenate(
        [nn(score_half, wide[:, 0:512]), nn(probs_half, wide[:, 512:1024])], axis=1
    )
    key_sum = nn(score_half, mask[:, 256:512])
    product = nn(turned, keys[:, 0:512])
    row_sum = jnp.sum(turned.astype(F32), axis=1, keepdims=True)
    query_part = jnp.zeros((ROWS, 512), F32)
    row_part = jnp.zeros((ROWS, 256), F32)
    for h in range(H):
        at = slice(h * ROWS, (h + 1) * ROWS)
        query_part = query_part + head_rows[at, :] * product[at, :]
        row_part = row_part + head_rows[at, 256:512] * row_sum[at, :]
    vectors = 0.25 * query_part[:, 0:256]
    points = (WC * point_gamma) * (query_part[:, 256:512] - features[:, 256:512] * row_part)
    points = pltpu.roll(points, 64, 1)
    query_out = jnp.concatenate(
        [vectors[:, :128], vectors[:, 128:] + points[:, :128], points[:, 128:]], axis=1
    )
    return key_part, key_sum, query_out


def sum_of(ref, count):
    total = ref[0].astype(F32)
    for k in range(1, count):
        total = total + ref[k].astype(F32)
    return total


def main_kernel(
    loss,
    residues,
    pair_hbm,
    queries_hbm,
    qpoints_hbm,
    frames_hbm,
    keyset_hbm,
    kpoints_hbm,
    values_hbm,
    vpoints_hbm,
    key_mask_hbm,
    weight_hbm,
    head_weight_hbm,
    gscalar_hbm,
    gpair_hbm,
    gpoints_hbm,
    pair_out,
    query_out,
    key_out,
    total_out,
    queries,
    qpoints,
    frames,
    keyset,
    kpoints,
    values,
    vpoints,
    key_mask,
    weight,
    head_weight,
    gscalar,
    gpair,
    gpoints,
    pair,
    blocks,
    own_block,
    pieces,
    own_piece,
    piece_rows,
    wide,
    mask,
    head_rows,
    expanded,
    placing,
    keys,
    square,
    weights,
    grads,
    distance,
    stats,
    arrived,
    answers,
    answered,
    table,
    halves,
    pair_stage,
    turned,
    flipped,
    key_acc,
    sum_acc,
    bias_acc,
    head_acc,
    query_parts,
    query_in,
    key_parts,
    key_in,
    totals,
    row_in,
    y_in,
    z_in,
    input_sem,
    pair_sem,
    own_sem,
    out_sem,
    send_sem,
    recv_sem,
    key_send,
    key_recv,
    stats_send,
    stats_recv,
    answer_send,
    answer_recv,
    query_send,
    query_recv,
    part_send,
    part_recv,
    total_send,
    total_recv,
):
    row, col = lax.axis_index("row"), lax.axis_index("col")
    z, y = col // 4, col % 4
    here = (row, col)
    groups = blocks.shape[0]

    def remote(source, target, send, recv, device):
        return pltpu.make_async_remote_copy(source, target, send, recv, device, MESH)

    barrier = pltpu.get_barrier_semaphore()
    for d in (1, 2, 3):
        pl.semaphore_signal(barrier, 1, device_id=(row, z * 4 + (y + d) % 4), device_id_type=MESH)
    for d in (1, 7):
        pl.semaphore_signal(
            barrier, 1, device_id=(row, ((z + d) % 8) * 4 + y), device_id_type=MESH
        )
    for d in range(1, 8):
        pl.semaphore_signal(barrier, 1, device_id=((row + d) % 8, col), device_id_type=MESH)
    inputs = (
        (queries_hbm, queries),
        (qpoints_hbm, qpoints),
        (frames_hbm, frames),
        (keyset_hbm, keyset),
        (kpoints_hbm, kpoints),
        (values_hbm, values),
        (vpoints_hbm, vpoints),
        (key_mask_hbm, key_mask),
        (weight_hbm, weight),
        (head_weight_hbm, head_weight),
        (gscalar_hbm, gscalar),
        (gpair_hbm, gpair),
        (gpoints_hbm, gpoints),
    )
    input_copies = []
    for k, (source, target) in enumerate(inputs):
        copy = pltpu.make_async_copy(source, target, input_sem.at[k])
        copy.start()
        input_copies.append(copy)
    quarter = pair.shape[0] // 4
    pair_copies = []
    for k in range(4):
        at = pl.ds(k * quarter, quarter)
        copy = pltpu.make_async_copy(pair_hbm.at[at], pair.at[at], pair_sem.at[k])
        copy.start()
        pair_copies.append(copy)
    for copy in input_copies:
        copy.wait()
    make_block(own_block, queries, qpoints, frames, gscalar, gpair, gpoints, wide, loss)
    make_key_piece(own_piece, keyset, kpoints, values, vpoints, piece_rows)
    pl.semaphore_wait(barrier, 12)

    up = (row, ((z + 1) % 8) * 4 + y)
    down = (row, ((z + 7) % 8) * 4 + y)

    def send_block(source, slot, target, at):
        remote(source, blocks.at[slot], send_sem.at[at], recv_sem.at[slot], target).start()

    def block_arrived(slot):
        remote(own_block, blocks.at[slot], send_sem.at[0], recv_sem.at[slot], here).wait_recv()

    send_block(own_block, col, up, 0)
    send_block(own_block, col, down, 1)
    for n, d in enumerate((1, 3, 2)):
        send_block(own_block, col, (row, z * 4 + (y + d) % 4), 2 + n)
    for d in range(1, 8):
        peer = ((row + d) % 8, col)
        remote(own_piece, pieces.at[row], key_send.at[d], key_recv.at[row], peer).start()
    own_copy = pltpu.make_async_copy(own_block, blocks.at[col], own_sem.at[0])
    own_copy.start()
    piece_copy = pltpu.make_async_copy(own_piece, pieces.at[row], own_sem.at[1])
    piece_copy.start()

    full = head_mask()
    mask[...] = full.astype(BF16)
    head_rows[...] = full[0 : H * ROWS, 0:512]
    fill_weight(expanded, weight[...])
    fill_placing(placing)
    key_acc[...] = jnp.zeros_like(key_acc)
    sum_acc[...] = jnp.zeros_like(sum_acc)
    bias_acc[...] = jnp.zeros_like(bias_acc)
    head_acc[...] = jnp.zeros_like(head_acc)
    masks = residue_masks()
    gamma = softplus_of(per_head(head_weight, lane_heads()))
    point_gamma = softplus_of(per_head(head_weight, feature_heads()[:, 256:512]))
    masking = 100000.0 * (1.0 - key_mask[...].astype(F32))
    masking = jnp.broadcast_to(masking, (ROWS, masking.shape[1])).T[:, 0:1]

    for n, d in enumerate((1, 3, 2)):
        slot = z * 4 + (y + d) % 4
        block_arrived(slot)
        send_block(blocks.at[slot], slot, up, 5 + 2 * n)
        send_block(blocks.at[slot], slot, down, 6 + 2 * n)
    for d in range(1, 8):
        source = (row + d) % 8
        remote(own_piece, pieces.at[source], key_send.at[d], key_recv.at[source], here).wait_recv()
    piece_copy.wait()
    own_copy.wait()
    tall = jnp.concatenate([pieces[r] for r in range(8)], axis=1)
    keys[...] = nn(tall, placing[...]).astype(BF16)
    points = keys[:, 256:512].astype(F32)
    squares = points * points
    high_part = squares.astype(BF16)
    low_part = (squares - high_part.astype(F32)).astype(BF16)
    square[...] = nt(high_part, mask[:, 256:512]) + nt(low_part, mask[:, 256:512])
    for copy in pair_copies:
        copy.wait()

    def send_stats(slot):
        remote(
            stats.at[slot], arrived.at[col], stats_send.at[slot], stats_recv.at[col], (row, slot)
        ).start()

    def forward_one(slot):
        first = pl.multiple_of(slot * ROWS, ROWS)
        pairs = jnp.concatenate([pair[first + i] for i in range(ROWS)], axis=1)
        out = forward_group(
            pairs, blocks[slot], masks, mask, expanded, keys, square, masking, gamma
        )
        weights[slot], grads[slot], distance[slot] = out[0], out[1], out[2]
        for n in range(3):
            stats[slot, :, n * LANES : (n + 1) * LANES] = out[3 + n]

    def forward_step(e, _):
        low, high = ring_slots(e, z, y)

        @pl.when(e >= 2)
        def _():
            block_arrived(low)

        @pl.when((e >= 2) & (e <= 11))
        def _():
            send_block(blocks.at[low], low, up, 11 + e)

        @pl.when(e >= 2)
        def _():
            block_arrived(high)

        @pl.when(((e >= 2) & (e <= 9)) | ((e >= 12) & (e <= 13)))
        def _():
            send_block(blocks.at[high], high, down, 23 + e)

        @pl.when(e >= 1)
        def _():
            send_stats(ring_slots(e - 1, z, y)[0])

        @pl.when(e >= 2)
        def _():
            send_stats(ring_slots(e - 1, z, y)[1])

        forward_one(low)
        forward_one(high)
        return 0

    lax.fori_loop(0, 16, forward_step, 0)
    arrived[col] = stats[col]
    for slot in ring_slots(15, z, y):
        send_stats(slot)

    def stats_arrived(d, _):
        peer = (col + d) % 32
        remote(
            stats.at[peer], arrived.at[peer], stats_send.at[peer], stats_recv.at[peer], here
        ).wait_recv()
        return 0

    lax.fori_loop(1, 32, stats_arrived, 0)
    combine_stats(arrived, answers, table)

    for d in range(16, 48):
        if d != 32:
            peer = (col + d) % 32
            remote(
                answers.at[peer],
                answered.at[col],
                answer_send.at[peer],
                answer_recv.at[col],
                (row, peer),
            ).start()
    answered[col] = answers[col]

    def score_one(slot, k):
        first = pl.multiple_of(slot * ROWS, ROWS)
        pairs = [pair[first + i] for i in range(ROWS)]
        score_half, probs_half, head_part = score_group(
            answered[slot, :, 0:LANES],
            answered[slot, :, LANES : 2 * LANES],
            weights[slot],
            grads[slot],
            distance[slot],
        )
        halves[slot, :, 0:LANES] = score_half
        halves[slot, :, LANES : 2 * LANES] = probs_half
        turned[slot], bias_part = bias_group(score_half, pairs, flipped.at[k])
        return bias_part, head_part

    def answer_arrived(slot):
        remote(
            answers.at[slot], answered.at[slot], answer_send.at[slot], answer_recv.at[slot], here
        ).wait_recv()

    def score_step(e, _):
        first, second = near_slot(2 * e, z, y), near_slot(2 * e + 1, z, y)

        @pl.when(e >= 1)
        def _():
            answer_arrived(first)

        answer_arrived(second)
        bias_a, head_a = score_one(first, 0)
        bias_b, head_b = score_one(second, 1)
        bias_acc[...] += bias_a + bias_b
        head_acc[...] += head_a + head_b
        return 0

    lax.fori_loop(0, 16, score_step, 0)
    totals[0, 0:16, :] = bias_acc[...]
    totals[0, 16:24, :] = jnp.broadcast_to(head_acc[...], (ROWS, LANES))

    def spread_total(source, target, me, count, base, device):
        for d in range(1, count):
            remote(
                source,
                target.at[me],
                total_send.at[base + d],
                total_recv.at[base + me],
                device((me + d) % count),
            ).start()

    def total_arrived(source, target, me, count, base):
        for d in range(1, count):
            peer = (me + d) % count
            remote(
                source, target.at[peer], total_send.at[base + d], total_recv.at[base + peer], here
            ).wait_recv()

    spread_total(totals.at[0], row_in, row, 8, 0, lambda p: (p, col))
    row_in[row] = totals[0]

    def send_query(slot):
        remote(
            query_parts.at[slot], query_in.at[col], query_send.at[slot], query_recv.at[col], (row, slot)
        ).start()

    def small_one(slot):
        out = small_group(
            halves[slot, :, 0:LANES],
            halves[slot, :, LANES : 2 * LANES],
            turned[slot],
            blocks[slot],
            mask,
            head_rows,
            keys,
            point_gamma,
        )
        query_parts[slot] = out[2].astype(BF16)
        return out[0], out[1]

    def small_step(e, _):
        first, second = near_slot(31 - 2 * e, z, y), near_slot(30 - 2 * e, z, y)

        @pl.when(e >= 1)
        def _():
            send_query(near_slot(33 - 2 * e, z, y))
            send_query(near_slot(32 - 2 * e, z, y))

        key_a, sum_a = small_one(first)
        key_b, sum_b = small_one(second)
        key_acc[...] += key_a + key_b
        sum_acc[...] += sum_a + sum_b
        return 0

    def stage_copy(slot):
        at = pl.ds(pl.multiple_of(slot * ROWS, ROWS), ROWS)
        return pltpu.make_async_copy(pair_stage.at[at], pair_out.at[at], out_sem.at[slot])

    def pair_step(e, _):
        @pl.when(e >= 1)
        def _():
            stage_copy(2 * e - 2).start()
            stage_copy(2 * e - 1).start()

        for k in range(2):
            slot = 2 * e + k
            first = pl.multiple_of(slot * ROWS, ROWS)
            side = jnp.concatenate([expanded[...], expanded_pairs(blocks[slot], masks)], axis=0)
            out = nn(halves[slot], side)
            for i in range(ROWS):
                pair_stage[first + i] = out[:, i * LANES : (i + 1) * LANES].astype(BF16)
        return 0

    lax.fori_loop(0, 8, small_step, 0)
    lax.fori_loop(0, 2, pair_step, 0)
    total_arrived(totals.at[0], row_in, row, 8, 0)
    totals[1] = sum_of(row_in, 8)
    y_in[y] = totals[1]
    spread_total(totals.at[1], y_in, y, 4, 8, lambda p: (row, z * 4 + p))
    lax.fori_loop(8, 16, small_step, 0)
    send_query(near_slot(1, z, y))
    query_in[col] = query_parts[col]
    total_arrived(totals.at[1], y_in, y, 4, 8)
    totals[2] = sum_of(y_in, 4)
    z_in[z] = totals[2]
    spread_total(totals.at[2], z_in, z, 8, 12, lambda p: (row, p * 4 + y))
    key_points = (WC * point_gamma) * (
        key_acc[:, 256:512] - keys[:, 256:512].astype(F32) * sum_acc[...]
    )
    whole = jnp.concatenate(
        [0.25 * key_acc[:, 0:256], key_points, key_acc[:, 512:1024]], axis=1
    ).astype(BF16)
    spread = nt(whole, placing[...])
    for r in range(8):
        key_parts[r] = spread[:, r * LANES : (r + 1) * LANES].astype(BF16)
    key_in[row] = key_parts[row]
    for d in range(1, 8):
        peer = (row + d) % 8
        remote(
            key_parts.at[peer], key_in.at[row], part_send.at[d], part_recv.at[row], (peer, col)
        ).start()

    lax.fori_loop(2, 16, pair_step, 0)

    def query_arrived(d, _):
        peer = (col + d) % 32
        remote(
            query_parts.at[peer], query_in.at[peer], query_send.at[peer], query_recv.at[peer], here
        ).wait_recv()
        return 0

    lax.fori_loop(1, 32, query_arrived, 0)
    mine = sum_of(query_in, 32)
    query_out[:, 0:256] = mine[:, 0:256]
    back = pltpu.roll(mine, 384 - 192, 1)[:, 0:256]
    lane = iota((ROWS, 256), 1)
    back = jnp.where(lane < 3.0 * H * PQ, back, 0.0)
    query_out[:, 256:512] = rotated(frames[...], back, 256, True)
    for d in range(1, 8):
        peer = (row + d) % 8
        remote(
            key_parts.at[peer], key_in.at[peer], part_send.at[d], part_recv.at[peer], here
        ).wait_recv()
    key_out[...] = sum_of(key_in, 8).T
    stage_copy(groups - 2).start()
    stage_copy(groups - 1).start()
    total_arrived(totals.at[2], z_in, z, 8, 12)
    total_out[...] = sum_of(z_in, 8)

    for at in list(range(11)) + list(range(13, 23)) + list(range(25, 33)) + [35, 36]:
        remote(own_block, blocks.at[0], send_sem.at[at], recv_sem.at[0], here).wait_send()
    for d in range(1, 8):
        remote(own_piece, pieces.at[0], key_send.at[d], key_recv.at[0], here).wait_send()
        remote(key_parts.at[0], key_in.at[0], part_send.at[d], part_recv.at[0], here).wait_send()

    def all_left(d, _):
        peer = (col + d) % 32
        remote(
            stats.at[peer], arrived.at[peer], stats_send.at[peer], stats_recv.at[peer], here
        ).wait_send()
        remote(
            answers.at[peer], answered.at[peer], answer_send.at[peer], answer_recv.at[peer], here
        ).wait_send()
        remote(
            query_parts.at[peer], query_in.at[peer], query_send.at[peer], query_recv.at[peer], here
        ).wait_send()
        return 0

    lax.fori_loop(1, 32, all_left, 0)
    for base, count in ((0, 8), (8, 4), (12, 8)):
        for d in range(1, count):
            remote(
                totals.at[0], row_in.at[0], total_send.at[base + d], total_recv.at[0], here
            ).wait_send()

    def stage_left(slot, _):
        stage_copy(slot).wait()
        return 0

    lax.fori_loop(0, groups, stage_left, 0)


def last_kernel(
    residues,
    pair_in,
    head_weight,
    query_sum,
    key_sum,
    total_sum,
    pair_grad,
    queries_grad,
    qpoints_grad,
    keyset_grad,
    kpoints_grad,
    values_grad,
    vpoints_grad,
    bias_grad,
    head_grad,
    stage,
    in_sem,
    out_sem,
):
    pieces = in_sem.shape[0]
    size = stage.shape[0] // pieces
    arrivals, leaves = [], []
    for k in range(pieces):
        at = pl.ds(k * size, size)
        arrivals.append(pltpu.make_async_copy(pair_in.at[at], stage.at[at], in_sem.at[k]))
        leaves.append(pltpu.make_async_copy(stage.at[at], pair_grad.at[at], out_sem.at[k]))
        arrivals[k].start()
    queries_grad[...] = query_sum[:, 0:192]
    qpoints_grad[...] = query_sum[:, 256:400]
    at = 0
    for out in (keyset_grad, kpoints_grad, values_grad, vpoints_grad):
        out[...] = key_sum[at : at + out.shape[0], :]
        at += out.shape[0]
    bias_grad[...] = total_sum[0:H, :] * (1.0 / residues)
    heads = lane_heads()
    raw = per_head(head_weight, heads)
    line = total_sum[16:17, :] * (-DIST_WEIGHT / residues) / (1.0 + jnp.exp(-raw))
    for h in range(H):
        head_grad[h] = jnp.sum(jnp.where(heads == float(h), line, 0.0))
    for k in range(pieces):
        arrivals[k].wait()
        leaves[k].start()
    for k in range(pieces):
        leaves[k].wait()


def shape(*dims, dtype=F32):
    return jax.ShapeDtypeStruct(dims, dtype)


VMEM = pl.BlockSpec(memory_space=pltpu.VMEM)
SMEM = pl.BlockSpec(memory_space=pltpu.SMEM)
ANY = pl.BlockSpec(memory_space=pl.ANY)
HBM = pl.BlockSpec(memory_space=pltpu.HBM)
DMA = pltpu.SemaphoreType.DMA


def local(
    pair_rep,
    queries,
    qpoints,
    frames,
    keyset,
    kpoints,
    values,
    vpoints,
    key_mask,
    bias_weight,
    head_weight,
    grad_scalar,
    grad_pair,
    grad_points,
):
    rows, keys, _ = pair_rep.shape
    residues = queries.shape[0] * 256
    loss = float(residues // 16)
    groups = rows // ROWS
    weight = bias_weight.T
    full, half = pltpu.VMEM, lambda *dims: pltpu.VMEM(dims, BF16)
    given = (
        queries,
        qpoints,
        frames,
        keyset.T,
        kpoints.T,
        values.T,
        vpoints.T,
        key_mask.reshape(1, keys),
        weight,
        head_weight.reshape(1, H),
        grad_scalar,
        grad_pair,
        grad_points,
    )
    pair_main, query_sum, key_sum, total_sum = pl.pallas_call(
        functools.partial(main_kernel, loss, float(residues)),
        out_shape=(
            shape(rows, keys, LANES, dtype=BF16),
            shape(ROWS, 512),
            shape(LANES, keys),
            shape(24, LANES),
        ),
        in_specs=[HBM] * (1 + len(given)),
        out_specs=(HBM, VMEM, VMEM, VMEM),
        scratch_shapes=[
            *(full(array.shape, array.dtype) for array in given),
            half(rows, keys, LANES),
            half(groups, 160, LANES),
            half(160, LANES),
            half(8, keys, LANES),
            half(keys, LANES),
            full((LANES, keys), F32),
            full((ROWS, 384), F32),
            half(LANES, FEATURES),
            full((H * ROWS, 512), F32),
            half(LANES, FEATURES),
            half(FEATURES, FEATURES),
            half(keys, FEATURES),
            full((keys, LANES), F32),
            full((groups, keys, LANES), F32),
            full((groups, keys, LANES), F32),
            full((groups, keys, LANES), F32),
            full((groups, 1, 3 * LANES), F32),
            full((groups, 1, 3 * LANES), F32),
            full((groups, 1, 2 * LANES), F32),
            full((groups, 1, 2 * LANES), F32),
            full((3, groups, LANES), F32),
            half(groups, keys, 2 * LANES),
            half(rows, keys, LANES),
            half(groups, LANES, keys),
            full((2, LANES, keys), F32),
            full((keys, FEATURES), F32),
            full((keys, 256), F32),
            full((16, LANES), F32),
            full((1, LANES), F32),
            half(groups, ROWS, 384),
            half(groups, ROWS, 384),
            half(8, keys, LANES),
            half(8, keys, LANES),
            full((3, 24, LANES), F32),
            full((8, 24, LANES), F32),
            full((4, 24, LANES), F32),
            full((8, 24, LANES), F32),
            DMA((len(given),)),
            DMA((4,)),
            DMA((2,)),
            DMA((groups,)),
            DMA((40,)),
            DMA((32,)),
            DMA((8,)),
            DMA((8,)),
            DMA((32,)),
            DMA((32,)),
            DMA((32,)),
            DMA((32,)),
            DMA((32,)),
            DMA((32,)),
            DMA((8,)),
            DMA((8,)),
            DMA((20,)),
            DMA((20,)),
        ],
        compiler_params=pltpu.CompilerParams(
            collective_id=0, has_side_effects=True, vmem_limit_bytes=67043328
        ),
        name="main",
    )(pair_rep, *given)
    finals = (
        (ROWS, H * C),
        (ROWS, 3 * H * PQ),
        (24, keys),
        (18, keys),
        (24, keys),
        (36, keys),
        (H, CZ),
    )
    pair_grad, queries_grad, qpoints_grad, *turned, bias_grad, head_grad = pl.pallas_call(
        functools.partial(last_kernel, float(residues)),
        out_shape=(
            shape(rows, keys, LANES, dtype=BF16),
            *(shape(*dims) for dims in finals),
            shape(H),
        ),
        in_specs=[HBM] + [VMEM] * 4,
        out_specs=(HBM,) + (VMEM,) * 7 + (SMEM,),
        scratch_shapes=[half(rows, keys, LANES), DMA((8,)), DMA((8,))],
        compiler_params=pltpu.CompilerParams(vmem_limit_bytes=67043328),
        name="last",
    )(pair_main, head_weight.reshape(1, H), query_sum, key_sum, total_sum)
    return (
        pair_grad,
        queries_grad,
        qpoints_grad,
        *(array.T for array in turned),
        bias_grad.T,
        head_grad,
    )


def solution(mesh):
    both = ("row", "col")
    return jax.shard_map(
        local,
        mesh=mesh,
        in_specs=(
            P("row", "col", None),
            P(both, None),
            P(both, None),
            P(both, None),
            P("col", "row"),
            P("col", "row"),
            P("col", "row"),
            P("col", "row"),
            P("col"),
            P(),
            P(),
            P(both, None),
            P(both, None),
            P(both, None),
        ),
        out_specs=(
            P("row", "col", None),
            P(both, None),
            P(both, None),
            P("col", "row"),
            P("col", "row"),
            P("col", "row"),
            P("col", "row"),
            P(),
            P(),
        ),
        check_vma=False,
    )
```

```python
import functools
import math

import jax
import jax.numpy as jnp
from jax import lax
from jax.experimental import pallas as pl
from jax.experimental.pallas import tpu as pltpu
from jax.sharding import PartitionSpec as P

H = 12
C = 16
CZ = 128
PQ = 4
PV = 8
LANES = 128
ROWS = 8
FEATURES = 1024
MESH = pl.DeviceIdType.MESH
F32 = jnp.float32
BF16 = jnp.bfloat16
WL = math.sqrt(1.0 / 3.0)
WC = math.sqrt(2.0 / (9.0 * PQ))
DIST_WEIGHT = 0.5 * WL * WC


def nt(a, b):
    return lax.dot_general(a, b, (((1,), (1,)), ((), ())), preferred_element_type=F32)


def nn(a, b):
    return lax.dot_general(a, b, (((1,), (0,)), ((), ())), preferred_element_type=F32)


def iota(shape, dim):
    return lax.broadcasted_iota(jnp.int32, shape, dim).astype(F32)


def whole_part(x, divisor):
    return jnp.floor((x + 0.5) * (1.0 / divisor))


def padded(scratch, array, width):
    rows, used = array.shape
    scratch[0:rows, 0:width] = jnp.zeros((rows, width), F32)
    scratch[0:rows, 0:used] = array.astype(F32)
    return scratch[0:rows, 0:width]


def rotated(frames, points, width, back):
    lane = iota((ROWS, width), 1)
    place = lane - 3.0 * whole_part(lane, 3)
    total = jnp.zeros((ROWS, width), F32)
    for step in range(-2, 3):
        factor = jnp.zeros((ROWS, width), F32)
        for a in range(3):
            b = a + step
            if 0 <= b < 3:
                at = 3 * b + a if back else 3 * a + b
                factor = jnp.where(place == float(a), frames[:, at : at + 1], factor)
        moved = points if step == 0 else pltpu.roll(points, (-step) % width, 1)
        total = total + factor * moved
    return total


def shifted(frames, width):
    lane = iota((ROWS, width), 1)
    place = lane - 3.0 * whole_part(lane, 3)
    total = jnp.zeros((ROWS, width), F32)
    for a in range(3):
        total = jnp.where(place == float(a), frames[:, 9 + a : 10 + a], total)
    return jnp.where(lane < 3.0 * H * PQ, total, 0.0)


def feature_heads():
    lane = iota((1, FEATURES), 1)
    heads = whole_part(lane, C)
    points = whole_part(lane - 256.0, 3 * PQ)
    scalars = whole_part(lane - 512.0, C)
    globals_ = whole_part(lane - 704.0, 3 * PV)
    none = jnp.full((1, FEATURES), 99.0, F32)
    heads = jnp.where(lane < 192.0, heads, none)
    heads = jnp.where((lane >= 256.0) & (lane < 400.0), points, heads)
    heads = jnp.where((lane >= 512.0) & (lane < 704.0), scalars, heads)
    return jnp.where((lane >= 704.0) & (lane < 992.0), globals_, heads)


def head_mask():
    row = whole_part(iota((LANES, FEATURES), 0), ROWS)
    return jnp.where(row == feature_heads(), 1.0, 0.0)


def fill_placing(placing):
    lane = iota((LANES, 1), 0)
    for r in range(8):
        place = jnp.full((LANES, 1), -1.0, F32)
        for first, width, base in ((0, 24, 0), (24, 18, 256), (42, 24, 512), (66, 36, 704)):
            inside = (lane >= float(first)) & (lane < float(first + width))
            place = jnp.where(inside, lane + float(base + r * width - first), place)
        at = iota((LANES, FEATURES), 1)
        placing[r * LANES : (r + 1) * LANES, :] = jnp.where(at == place, 1.0, 0.0).astype(BF16)


def per_head(values, heads):
    total = jnp.zeros(heads.shape, F32)
    for h in range(H):
        total = jnp.where(heads == float(h), values[:, h : h + 1], total)
    return total


def softplus_of(x):
    return jnp.log(1.0 + jnp.exp(x))


def lane_heads():
    return whole_part(iota((1, LANES), 1), ROWS)


def fill_weight(expanded, bias_weight):
    row = whole_part(iota((LANES, H), 0), ROWS)
    pick = jnp.where(row == iota((LANES, H), 1), 1.0, 0.0).astype(BF16)
    rows = nn(pick, bias_weight)
    residue = iota((LANES, LANES), 0)
    residue = residue - ROWS * whole_part(residue, ROWS)
    for i in range(ROWS):
        expanded[:, i * LANES : (i + 1) * LANES] = jnp.where(
            residue == float(i), rows, 0.0
        ).astype(BF16)


def residue_masks():
    row = iota((H * ROWS, LANES), 0)
    row = row - ROWS * whole_part(row, ROWS)
    return [jnp.where(row == float(i), 1.0, 0.0).astype(BF16) for i in range(ROWS)]


def expanded_pairs(block, masks):
    pairs = block[0 : H * ROWS, :]
    wide = jnp.concatenate([pairs * m for m in masks], axis=1)
    return jnp.concatenate([wide, jnp.zeros((LANES - H * ROWS, FEATURES), BF16)], axis=0)


def expanded_features(features, mask):
    twice = jnp.concatenate([features, features], axis=0).astype(BF16)
    return jnp.concatenate([twice] * ROWS, axis=0) * mask


def wide_features(block):
    tall = block[H * ROWS :, :].astype(F32)
    return jnp.concatenate([tall[t * ROWS : (t + 1) * ROWS] for t in range(ROWS)], axis=1)


def packed(vectors, points):
    points = pltpu.roll(points, 64, 1)
    return jnp.concatenate(
        [vectors[:, :128], vectors[:, 128:] + points[:, :128], points[:, 128:]], axis=1
    )


def squared_lengths(points):
    lane = iota((LANES, 256), 1)
    row = whole_part(iota((LANES, 256), 0), ROWS)
    hit = (whole_part(lane, 3 * PQ) == row) & (lane < 3.0 * H * PQ)
    pick = jnp.where(hit, 1.0, 0.0).astype(BF16)
    points = points.astype(BF16).astype(F32)
    squares = points * points
    high = squares.astype(BF16).astype(F32)
    parts = jnp.concatenate(
        [expanded_features(high, pick), expanded_features(squares - high, pick)], axis=1
    )
    total = nt(jnp.ones((ROWS, 512), BF16), parts)
    first = total.astype(BF16).astype(F32)
    second = (total - first).astype(BF16).astype(F32)
    third = (total - first - second).astype(BF16).astype(F32)
    which = iota((ROWS, LANES), 0)
    rows = jnp.where(which == 0.0, first, jnp.where(which == 1.0, second, third))
    return pltpu.roll(jnp.where(which < 3.0, rows, 0.0), 16, 1)


def make_block(block, queries, qpoints, frames, gscalar, gpair, gpoints, wide, loss):
    f = frames[...]
    q = padded(wide, queries[...], 256)
    points = padded(wide, qpoints[...], 256)
    qg = rotated(f, points, 256, False) + shifted(f, 256)
    gs = padded(wide, gscalar[...], 256) * loss
    gg = rotated(f, padded(wide, gpoints[...], 384) * loss, 384, False)
    gg = pltpu.roll(gg, 64, 1)
    lengths = squared_lengths(qg)
    tiles = [q[:, :128], q[:, 128:], qg[:, :128], qg[:, 128:] + lengths, gs[:, :128]]
    tiles += [gs[:, 128:] + gg[:, :128], gg[:, 128:256], gg[:, 256:]]
    pairs = gpair[...].astype(F32) * loss
    tall = [pairs[:, h * CZ : (h + 1) * CZ] for h in range(H)]
    block[...] = jnp.concatenate(tall + tiles, axis=0).astype(BF16)


def make_key_piece(piece, keyset, kpoints, values, vpoints, tall):
    at = 0
    tall[...] = jnp.zeros_like(tall)
    for array in (keyset, kpoints, values, vpoints):
        tall[at : at + array.shape[0], :] = array[...].astype(F32)
        at += array.shape[0]
    piece[...] = tall[...].T.astype(BF16)


def gray(i):
    return i + (i // 2) * (1 - 2 * (i % 2))


def ring_slots(e, z, y):
    s, i = (e + 2) // 4, (e + 2) % 4
    turn = s // 4 + (4 - s) // 4
    low = ((z + 8 - s) % 8) * 4 + (y + gray(i)) % 4
    high = ((z + s) % 8) * 4 + (y + gray((i + 2 * turn) % 4)) % 4
    return low, high


def near_slot(n, z, y):
    m, i = n // 4, n % 4
    dz = ((m + 1) // 2) * (2 * (m % 2) - 1)
    return ((z + 8 + dz) % 8) * 4 + (y + gray(i)) % 4


def forward_groups(pairs, blocks, masks, mask, expanded, keys, square, masking, gamma):
    rows = keys.shape[0]
    biases = nt(jnp.concatenate(pairs, axis=0), expanded[...])
    outs = []
    for k, block in enumerate(blocks):
        features = wide_features(block)
        wide = expanded_features(features, mask[...])
        bias = biases[k * rows : (k + 1) * rows, :]
        dots = nt(keys[:, 0:256], wide[:, 0:256])
        cross = nt(keys[:, 256:512], wide[:, 256:512])
        grads = nt(keys[:, 512:1024], wide[:, 512:1024]) + nt(
            pairs[k], expanded_pairs(block, masks)
        )
        line = features[0:1, 384:512] + features[1:2, 384:512] + features[2:3, 384:512]
        query_square = pltpu.roll(line, LANES - 16, 1)
        distance = query_square + square[...] - 2.0 * cross
        scores = WL * (dots * 0.25 + bias) - (DIST_WEIGHT * gamma) * distance - masking
        top = jnp.max(scores, axis=0, keepdims=True)
        weights = jnp.exp(scores - top)
        total = jnp.sum(weights, axis=0, keepdims=True)
        inner = jnp.sum(weights * grads, axis=0, keepdims=True)
        outs.append((weights, grads, distance, top, total, inner))
    return outs


def combine_stats(arrived, answers, table):
    for d in range(32):
        for n in range(3):
            table[n, d : d + 1, :] = arrived[d, :, n * LANES : (n + 1) * LANES]
    tops = table[0]
    top = jnp.max(tops, axis=0, keepdims=True)
    factors = jnp.exp(tops - top)
    total = jnp.sum(factors * table[1], axis=0, keepdims=True)
    inner = jnp.sum(factors * table[2], axis=0, keepdims=True) / total
    factors = factors / total
    for d in range(32):
        answers[d, :, 0:LANES] = factors[d : d + 1, :]
        answers[d, :, LANES : 2 * LANES] = inner


def score_group(factor, inner, weights, grads, distance):
    probs = weights * factor
    score = probs * (grads - inner)
    head_part = jnp.sum(score * distance, axis=0, keepdims=True)
    return (WL * score).astype(BF16), probs.astype(BF16), head_part


def bias_group(score_half, pairs, flipped):
    turned = score_half.astype(F32).T
    flipped[...] = turned
    bias_part = jnp.zeros((16, LANES), F32)
    for i in range(ROWS):
        rows = flipped[pl.ds(i, 16, stride=ROWS), :].astype(BF16)
        bias_part = bias_part + nn(rows, pairs[i])
    return turned.astype(BF16), bias_part


def query_group(turned, features, head_rows, packed_keys, scale, point_scale):
    product = nn(turned, packed_keys)
    row_sum = jnp.sum(turned.astype(F32), axis=1, keepdims=True)
    query_part = jnp.zeros((ROWS, 384), F32)
    row_part = jnp.zeros((ROWS, 256), F32)
    for h in range(H):
        at = slice(h * ROWS, (h + 1) * ROWS)
        query_part = query_part + head_rows[at, 0:384] * product[at, :]
        row_part = row_part + head_rows[at, 384:640] * row_sum[at, :]
    less = point_scale * pltpu.roll(features[:, 256:512], 64, 1) * row_part
    query_part = scale * query_part
    return jnp.concatenate([query_part[:, :128], query_part[:, 128:] - less], axis=1)


def sum_of(ref, count):
    total = ref[0].astype(F32)
    for k in range(1, count):
        total = total + ref[k].astype(F32)
    return total


def main_kernel(
    loss,
    residues,
    pair_hbm,
    queries_hbm,
    qpoints_hbm,
    frames_hbm,
    keyset_hbm,
    kpoints_hbm,
    values_hbm,
    vpoints_hbm,
    key_mask_hbm,
    weight_hbm,
    head_weight_hbm,
    gscalar_hbm,
    gpair_hbm,
    gpoints_hbm,
    pair_out,
    query_out,
    key_out,
    total_out,
    queries,
    qpoints,
    frames,
    keyset,
    kpoints,
    values,
    vpoints,
    key_mask,
    weight,
    head_weight,
    gscalar,
    gpair,
    gpoints,
    pair,
    blocks,
    own_block,
    pieces,
    own_piece,
    piece_rows,
    wide,
    mask,
    head_rows,
    expanded,
    placing,
    keys,
    packed_keys,
    square,
    weights,
    grads,
    distance,
    stats,
    arrived,
    answers,
    answered,
    table,
    halves,
    pair_stage,
    turned,
    flipped,
    key_acc,
    sum_acc,
    bias_acc,
    head_acc,
    query_parts,
    query_in,
    key_parts,
    key_in,
    totals,
    row_in,
    y_in,
    z_in,
    input_sem,
    pair_sem,
    own_sem,
    out_sem,
    send_sem,
    upper_recv,
    lower_recv,
    key_send,
    key_recv,
    stats_send,
    stats_recv,
    answer_send,
    answer_recv,
    query_send,
    query_recv,
    part_send,
    part_recv,
    total_send,
    total_recv,
):
    row, col = lax.axis_index("row"), lax.axis_index("col")
    z, y = col // 4, col % 4
    here = (row, col)
    groups = blocks.shape[0]

    def remote(source, target, send, recv, device):
        return pltpu.make_async_remote_copy(source, target, send, recv, device, MESH)

    barrier = pltpu.get_barrier_semaphore()
    for d in (1, 2, 3):
        pl.semaphore_signal(barrier, 1, device_id=(row, z * 4 + (y + d) % 4), device_id_type=MESH)
    for d in (1, 7):
        pl.semaphore_signal(
            barrier, 1, device_id=(row, ((z + d) % 8) * 4 + y), device_id_type=MESH
        )
    for d in range(1, 8):
        pl.semaphore_signal(barrier, 1, device_id=((row + d) % 8, col), device_id_type=MESH)
    inputs = (
        (queries_hbm, queries),
        (qpoints_hbm, qpoints),
        (frames_hbm, frames),
        (keyset_hbm, keyset),
        (kpoints_hbm, kpoints),
        (values_hbm, values),
        (vpoints_hbm, vpoints),
        (key_mask_hbm, key_mask),
        (weight_hbm, weight),
        (head_weight_hbm, head_weight),
        (gscalar_hbm, gscalar),
        (gpair_hbm, gpair),
        (gpoints_hbm, gpoints),
    )
    input_copies = []
    for k, (source, target) in enumerate(inputs):
        copy = pltpu.make_async_copy(source, target, input_sem.at[k])
        copy.start()
        input_copies.append(copy)
    quarter = pair.shape[0] // 4
    pair_copies = []
    for k in range(4):
        at = pl.ds(k * quarter, quarter)
        copy = pltpu.make_async_copy(pair_hbm.at[at], pair.at[at], pair_sem.at[k])
        copy.start()
        pair_copies.append(copy)
    for copy in input_copies:
        copy.wait()
    make_block(own_block, queries, qpoints, frames, gscalar, gpair, gpoints, wide, loss)
    make_key_piece(own_piece, keyset, kpoints, values, vpoints, piece_rows)
    pl.semaphore_wait(barrier, 12)

    up = (row, ((z + 1) % 8) * 4 + y)
    down = (row, ((z + 7) % 8) * 4 + y)

    parts = ((pl.ds(0, 160), upper_recv),)

    def send_part(source, slot, target, part):
        at, recv = part
        remote(source.at[at], blocks.at[slot, at], send_sem, recv.at[slot], target).start()

    def part_arrived(slot, part):
        at, recv = part
        remote(own_block.at[at], blocks.at[slot, at], send_sem, recv.at[slot], here).wait_recv()

    for part in parts:
        send_part(own_block, col, up, part)
        send_part(own_block, col, down, part)
        for d in (1, 3, 2):
            send_part(own_block, col, (row, z * 4 + (y + d) % 4), part)
    for d in range(1, 8):
        peer = ((row + d) % 8, col)
        remote(own_piece, pieces.at[row], key_send.at[d], key_recv.at[row], peer).start()
    own_copy = pltpu.make_async_copy(own_block, blocks.at[col], own_sem.at[0])
    own_copy.start()
    piece_copy = pltpu.make_async_copy(own_piece, pieces.at[row], own_sem.at[1])
    piece_copy.start()

    full = head_mask()
    mask[...] = full.astype(BF16)
    head_rows[:, 0:384] = packed(full[0 : H * ROWS, 0:256], full[0 : H * ROWS, 256:512])
    head_rows[:, 384:640] = pltpu.roll(full[0 : H * ROWS, 256:512], 64, 1)
    fill_weight(expanded, weight[...])
    fill_placing(placing)
    key_acc[...] = jnp.zeros_like(key_acc)
    sum_acc[...] = jnp.zeros_like(sum_acc)
    bias_acc[...] = jnp.zeros_like(bias_acc)
    head_acc[...] = jnp.zeros_like(head_acc)
    masks = residue_masks()
    gamma = softplus_of(per_head(head_weight, lane_heads()))
    point_gamma = softplus_of(per_head(head_weight, feature_heads()[:, 256:512]))
    vector_scale = jnp.where(iota((1, 256), 1) < 1.0 * H * C, 0.25, 0.0)
    used = jnp.where(iota((1, 256), 1) < 3.0 * H * PQ, WC * point_gamma, 0.0)
    scale = packed(vector_scale, used)
    point_scale = pltpu.roll(used, 64, 1)
    masking = 100000.0 * (1.0 - key_mask[...].astype(F32))
    masking = jnp.broadcast_to(masking, (ROWS, masking.shape[1])).T[:, 0:1]

    for d in (1, 3, 2):
        slot = z * 4 + (y + d) % 4
        for part in parts:
            part_arrived(slot, part)
            send_part(blocks.at[slot], slot, up, part)
            send_part(blocks.at[slot], slot, down, part)
    for d in range(1, 8):
        source = (row + d) % 8
        remote(own_piece, pieces.at[source], key_send.at[d], key_recv.at[source], here).wait_recv()
    piece_copy.wait()
    own_copy.wait()
    tall = jnp.concatenate([pieces[r] for r in range(8)], axis=1)
    keys[...] = nn(tall, placing[...]).astype(BF16)
    points = keys[:, 256:512].astype(F32)
    packed_keys[...] = packed(keys[:, 0:256].astype(F32), points).astype(BF16)
    squares = points * points
    high_part = squares.astype(BF16)
    low_part = (squares - high_part.astype(F32)).astype(BF16)
    square[...] = nt(high_part, mask[:, 256:512]) + nt(low_part, mask[:, 256:512])
    for copy in pair_copies:
        copy.wait()

    def send_stats(slot):
        remote(
            stats.at[slot], arrived.at[col], stats_send, stats_recv, (row, slot)
        ).start()

    def pairs_of(slot):
        first = pl.multiple_of(slot * ROWS, ROWS)
        return [pair[first + i] for i in range(ROWS)]

    def forward_two(slots):
        pairs = [jnp.concatenate(pairs_of(slot), axis=1) for slot in slots]
        outs = forward_groups(
            pairs,
            [blocks[slot] for slot in slots],
            masks,
            mask,
            expanded,
            keys,
            square,
            masking,
            gamma,
        )
        for slot, out in zip(slots, outs):
            weights[slot], grads[slot], distance[slot] = out[0], out[1], out[2]
            for n in range(3):
                stats[slot, :, n * LANES : (n + 1) * LANES] = out[3 + n]

    def forward_step(e, _):
        low, high = ring_slots(e, z, y)

        for part in parts:

            @pl.when(e >= 2)
            def _(part=part):
                part_arrived(low, part)

            @pl.when((e >= 2) & (e <= 11))
            def _(part=part):
                send_part(blocks.at[low], low, up, part)

            @pl.when(e >= 2)
            def _(part=part):
                part_arrived(high, part)

            @pl.when(((e >= 2) & (e <= 9)) | ((e >= 12) & (e <= 13)))
            def _(part=part):
                send_part(blocks.at[high], high, down, part)

        @pl.when(e >= 1)
        def _():
            send_stats(ring_slots(e - 1, z, y)[0])

        @pl.when(e >= 2)
        def _():
            send_stats(ring_slots(e - 1, z, y)[1])

        forward_two((low, high))
        return 0

    lax.fori_loop(0, 16, forward_step, 0)
    arrived[col] = stats[col]
    for slot in ring_slots(15, z, y):
        send_stats(slot)

    most = pl.ds(0, groups - 1)

    def all_of(buffer, sem):
        pltpu.make_async_copy(buffer.at[most], buffer.at[most], sem).wait()

    all_of(arrived, stats_recv)
    combine_stats(arrived, answers, table)

    for d in range(16, 48):
        if d != 32:
            peer = (col + d) % 32
            remote(
                answers.at[peer],
                answered.at[col],
                answer_send,
                answer_recv.at[col],
                (row, peer),
            ).start()
    answered[col] = answers[col]

    def score_one(slot, k):
        pairs = pairs_of(slot)
        score_half, probs_half, head_part = score_group(
            answered[slot, :, 0:LANES],
            answered[slot, :, LANES : 2 * LANES],
            weights[slot],
            grads[slot],
            distance[slot],
        )
        halves[slot, :, 0:LANES] = score_half
        halves[slot, :, LANES : 2 * LANES] = probs_half
        turned[slot], bias_part = bias_group(score_half, pairs, flipped.at[k])
        return bias_part, head_part

    def answer_arrived(slot):
        remote(
            answers.at[slot], answered.at[slot], answer_send, answer_recv.at[slot], here
        ).wait_recv()

    def score_step(e, _):
        first, second = near_slot(2 * e, z, y), near_slot(2 * e + 1, z, y)

        @pl.when(e >= 1)
        def _():
            answer_arrived(first)

        answer_arrived(second)
        bias_a, head_a = score_one(first, 0)
        bias_b, head_b = score_one(second, 1)
        bias_acc[...] += bias_a + bias_b
        head_acc[...] += head_a + head_b
        return 0

    lax.fori_loop(0, 16, score_step, 0)
    totals[0, :, :] = bias_acc[...]
    totals[0, H : H + 1, :] = head_acc[...]

    def spread_total(source, target, me, count, base, device):
        for d in range(1, count):
            remote(
                source,
                target.at[me],
                total_send.at[base + d],
                total_recv.at[base + me],
                device((me + d) % count),
            ).start()

    def total_arrived(source, target, me, count, base):
        for d in range(1, count):
            peer = (me + d) % count
            remote(
                source, target.at[peer], total_send.at[base + d], total_recv.at[base + peer], here
            ).wait_recv()

    spread_total(totals.at[0], row_in, row, 8, 0, lambda p: (p, col))
    row_in[row] = totals[0]

    def send_query(slot):
        remote(
            query_parts.at[slot], query_in.at[col], query_send, query_recv, (row, slot)
        ).start()

    def small_two(slots):
        wides = []
        for slot in slots:
            features = wide_features(blocks[slot])
            wides.append(expanded_features(features, mask[...]))
            query_parts[slot] = query_group(
                turned[slot], features, head_rows, packed_keys[...], scale, point_scale
            ).astype(BF16)
        wide = jnp.concatenate(wides, axis=0)
        scores = [halves[slot, :, 0:LANES] for slot in slots]
        probs = [halves[slot, :, LANES : 2 * LANES] for slot in slots]
        key_acc[:, 0:512] += nn(jnp.concatenate(scores, axis=1), wide[:, 0:512])
        key_acc[:, 512:1024] += nn(jnp.concatenate(probs, axis=1), wide[:, 512:1024])
        sum_acc[...] += scores[0].astype(F32) + scores[1].astype(F32)

    def small_step(e, _):
        first, second = near_slot(31 - 2 * e, z, y), near_slot(30 - 2 * e, z, y)

        @pl.when(e >= 1)
        def _():
            send_query(near_slot(33 - 2 * e, z, y))
            send_query(near_slot(32 - 2 * e, z, y))

        small_two((first, second))
        return 0

    def stage_copy(slot):
        at = pl.ds(pl.multiple_of(slot * ROWS, ROWS), ROWS)
        return pltpu.make_async_copy(pair_stage.at[at], pair_out.at[at], out_sem)

    def pair_step(e, _):
        @pl.when(e >= 1)
        def _():
            stage_copy(2 * e - 2).start()
            stage_copy(2 * e - 1).start()

        for k in range(2):
            slot = 2 * e + k
            first = pl.multiple_of(slot * ROWS, ROWS)
            side = jnp.concatenate([expanded[...], expanded_pairs(blocks[slot], masks)], axis=0)
            out = nn(halves[slot], side)
            for i in range(ROWS):
                pair_stage[first + i] = out[:, i * LANES : (i + 1) * LANES].astype(BF16)
        return 0

    lax.fori_loop(0, 8, small_step, 0)
    lax.fori_loop(0, 2, pair_step, 0)
    total_arrived(totals.at[0], row_in, row, 8, 0)
    totals[1] = sum_of(row_in, 8)
    y_in[y] = totals[1]
    spread_total(totals.at[1], y_in, y, 4, 8, lambda p: (row, z * 4 + p))
    lax.fori_loop(8, 16, small_step, 0)
    send_query(near_slot(1, z, y))
    query_in[col] = query_parts[col]
    total_arrived(totals.at[1], y_in, y, 4, 8)
    totals[2] = sum_of(y_in, 4)
    z_in[z] = totals[2]
    spread_total(totals.at[2], z_in, z, 8, 12, lambda p: (row, p * 4 + y))
    sum_high = sum_acc[...].astype(BF16)
    sum_low = (sum_acc[...] - sum_high.astype(F32)).astype(BF16)
    key_sum = nn(sum_high, mask[:, 256:512]) + nn(sum_low, mask[:, 256:512])
    key_points = (WC * point_gamma) * (
        key_acc[:, 256:512] - keys[:, 256:512].astype(F32) * key_sum
    )
    whole = jnp.concatenate(
        [0.25 * key_acc[:, 0:256], key_points, key_acc[:, 512:1024]], axis=1
    ).astype(BF16)
    spread = nt(whole, placing[...])
    for r in range(8):
        key_parts[r] = spread[:, r * LANES : (r + 1) * LANES].astype(BF16)
    key_in[row] = key_parts[row]
    for d in range(1, 8):
        peer = (row + d) % 8
        remote(
            key_parts.at[peer], key_in.at[row], part_send.at[d], part_recv.at[row], (peer, col)
        ).start()

    lax.fori_loop(2, 16, pair_step, 0)

    all_of(query_in, query_recv)
    mine = sum_of(query_in, 32)
    query_out[:, 0:256] = mine[:, 0:256]
    back = pltpu.roll(mine, 384 - 192, 1)[:, 0:256]
    lane = iota((ROWS, 256), 1)
    back = jnp.where(lane < 3.0 * H * PQ, back, 0.0)
    query_out[:, 256:512] = rotated(frames[...], back, 256, True)
    for d in range(1, 8):
        peer = (row + d) % 8
        remote(
            key_parts.at[peer], key_in.at[peer], part_send.at[d], part_recv.at[peer], here
        ).wait_recv()
    key_out[...] = sum_of(key_in, 8).T
    stage_copy(groups - 2).start()
    stage_copy(groups - 1).start()
    total_arrived(totals.at[2], z_in, z, 8, 12)
    total_out[...] = sum_of(z_in, 8)

    all_of(blocks, send_sem)
    for d in range(1, 8):
        remote(own_piece, pieces.at[0], key_send.at[d], key_recv.at[0], here).wait_send()
        remote(key_parts.at[0], key_in.at[0], part_send.at[d], part_recv.at[0], here).wait_send()

    all_of(arrived, stats_send)
    all_of(answers, answer_send)
    all_of(query_in, query_send)
    for base, count in ((0, 8), (8, 4), (12, 8)):
        for d in range(1, count):
            remote(
                totals.at[0], row_in.at[0], total_send.at[base + d], total_recv.at[0], here
            ).wait_send()

    pltpu.make_async_copy(pair_stage, pair_out, out_sem).wait()


def last_kernel(
    residues,
    pair_in,
    head_weight,
    query_sum,
    key_sum,
    total_sum,
    pair_grad,
    queries_grad,
    qpoints_grad,
    keyset_grad,
    kpoints_grad,
    values_grad,
    vpoints_grad,
    bias_grad,
    head_grad,
    stage,
    in_sem,
    out_sem,
):
    pieces = in_sem.shape[0]
    size = stage.shape[0] // pieces
    arrivals, leaves = [], []
    for k in range(pieces):
        at = pl.ds(k * size, size)
        arrivals.append(pltpu.make_async_copy(pair_in.at[at], stage.at[at], in_sem.at[k]))
        leaves.append(pltpu.make_async_copy(stage.at[at], pair_grad.at[at], out_sem.at[k]))
        arrivals[k].start()
    queries_grad[...] = query_sum[:, 0:192]
    qpoints_grad[...] = query_sum[:, 256:400]
    at = 0
    for out in (keyset_grad, kpoints_grad, values_grad, vpoints_grad):
        out[...] = key_sum[at : at + out.shape[0], :]
        at += out.shape[0]
    bias_grad[...] = total_sum[0:H, :] * (1.0 / residues)
    heads = lane_heads()
    raw = per_head(head_weight, heads)
    line = total_sum[H : H + 1, :] * (-DIST_WEIGHT / residues) / (1.0 + jnp.exp(-raw))
    for h in range(H):
        head_grad[h] = jnp.sum(jnp.where(heads == float(h), line, 0.0))
    for k in range(pieces):
        arrivals[k].wait()
        leaves[k].start()
    for k in range(pieces):
        leaves[k].wait()


def shape(*dims, dtype=F32):
    return jax.ShapeDtypeStruct(dims, dtype)


VMEM = pl.BlockSpec(memory_space=pltpu.VMEM)
SMEM = pl.BlockSpec(memory_space=pltpu.SMEM)
ANY = pl.BlockSpec(memory_space=pl.ANY)
HBM = pl.BlockSpec(memory_space=pltpu.HBM)
DMA = pltpu.SemaphoreType.DMA


def local(
    pair_rep,
    queries,
    qpoints,
    frames,
    keyset,
    kpoints,
    values,
    vpoints,
    key_mask,
    bias_weight,
    head_weight,
    grad_scalar,
    grad_pair,
    grad_points,
):
    rows, keys, _ = pair_rep.shape
    residues = queries.shape[0] * 256
    loss = float(residues // 16)
    groups = rows // ROWS
    weight = bias_weight.T
    full, half = pltpu.VMEM, lambda *dims: pltpu.VMEM(dims, BF16)
    given = (
        queries,
        qpoints,
        frames,
        keyset.T,
        kpoints.T,
        values.T,
        vpoints.T,
        key_mask.reshape(1, keys),
        weight,
        head_weight.reshape(1, H),
        grad_scalar,
        grad_pair,
        grad_points,
    )
    pair_main, query_sum, key_sum, total_sum = pl.pallas_call(
        functools.partial(main_kernel, loss, float(residues)),
        out_shape=(
            shape(rows, keys, LANES, dtype=BF16),
            shape(ROWS, 512),
            shape(LANES, keys),
            shape(16, LANES),
        ),
        in_specs=[HBM] * (1 + len(given)),
        out_specs=(HBM, VMEM, VMEM, VMEM),
        scratch_shapes=[
            *(full(array.shape, array.dtype) for array in given),
            half(rows, keys, LANES),
            half(groups, 160, LANES),
            half(160, LANES),
            half(8, keys, LANES),
            half(keys, LANES),
            full((LANES, keys), F32),
            full((ROWS, 384), F32),
            half(LANES, FEATURES),
            full((H * ROWS, 640), F32),
            half(LANES, FEATURES),
            half(FEATURES, FEATURES),
            half(keys, FEATURES),
            half(keys, 384),
            full((keys, LANES), F32),
            full((groups, keys, LANES), F32),
            full((groups, keys, LANES), F32),
            full((groups, keys, LANES), F32),
            full((groups, 1, 3 * LANES), F32),
            full((groups, 1, 3 * LANES), F32),
            full((groups, 1, 2 * LANES), F32),
            full((groups, 1, 2 * LANES), F32),
            full((3, groups, LANES), F32),
            half(groups, keys, 2 * LANES),
            half(rows, keys, LANES),
            half(groups, LANES, keys),
            full((2, LANES, keys), F32),
            full((keys, FEATURES), F32),
            full((keys, LANES), F32),
            full((16, LANES), F32),
            full((1, LANES), F32),
            half(groups, ROWS, 384),
            half(groups, ROWS, 384),
            half(8, keys, LANES),
            half(8, keys, LANES),
            full((3, 16, LANES), F32),
            full((8, 16, LANES), F32),
            full((4, 16, LANES), F32),
            full((8, 16, LANES), F32),
            DMA((len(given),)),
            DMA((4,)),
            DMA((2,)),
            DMA,
            DMA,
            DMA((groups,)),
            DMA((groups,)),
            DMA((8,)),
            DMA((8,)),
            DMA,
            DMA,
            DMA,
            DMA((groups,)),
            DMA,
            DMA,
            DMA((8,)),
            DMA((8,)),
            DMA((20,)),
            DMA((20,)),
        ],
        compiler_params=pltpu.CompilerParams(
            collective_id=0, has_side_effects=True, vmem_limit_bytes=67043328
        ),
        name="main",
    )(pair_rep, *given)
    finals = (
        (ROWS, H * C),
        (ROWS, 3 * H * PQ),
        (24, keys),
        (18, keys),
        (24, keys),
        (36, keys),
        (H, CZ),
    )
    pair_grad, queries_grad, qpoints_grad, *turned, bias_grad, head_grad = pl.pallas_call(
        functools.partial(last_kernel, float(residues)),
        out_shape=(
            shape(rows, keys, LANES, dtype=BF16),
            *(shape(*dims) for dims in finals),
            shape(H),
        ),
        in_specs=[HBM] + [VMEM] * 4,
        out_specs=(HBM,) + (VMEM,) * 7 + (SMEM,),
        scratch_shapes=[half(rows, keys, LANES), DMA((8,)), DMA((8,))],
        compiler_params=pltpu.CompilerParams(vmem_limit_bytes=67043328),
        name="last",
    )(pair_main, head_weight.reshape(1, H), query_sum, key_sum, total_sum)
    return (
        pair_grad,
        queries_grad,
        qpoints_grad,
        *(array.T for array in turned),
        bias_grad.T,
        head_grad,
    )


def solution(mesh):
    both = ("row", "col")
    return jax.shard_map(
        local,
        mesh=mesh,
        in_specs=(
            P("row", "col", None),
            P(both, None),
            P(both, None),
            P(both, None),
            P("col", "row"),
            P("col", "row"),
            P("col", "row"),
            P("col", "row"),
            P("col"),
            P(),
            P(),
            P(both, None),
            P(both, None),
            P(both, None),
        ),
        out_specs=(
            P("row", "col", None),
            P(both, None),
            P(both, None),
            P("col", "row"),
            P("col", "row"),
            P("col", "row"),
            P("col", "row"),
            P(),
            P(),
        ),
        check_vma=False,
    )
```

```python
import functools
import math

import jax
import jax.numpy as jnp
from jax import lax
from jax.experimental import pallas as pl
from jax.experimental.pallas import tpu as pltpu
from jax.sharding import PartitionSpec as P

H = 12
C = 16
CZ = 128
PQ = 4
PV = 8
LANES = 128
ROWS = 8
FEATURES = 1024
MESH = pl.DeviceIdType.MESH
F32 = jnp.float32
BF16 = jnp.bfloat16
WL = math.sqrt(1.0 / 3.0)
WC = math.sqrt(2.0 / (9.0 * PQ))
DIST_WEIGHT = 0.5 * WL * WC


def nt(a, b):
    return lax.dot_general(a, b, (((1,), (1,)), ((), ())), preferred_element_type=F32)


def nn(a, b):
    return lax.dot_general(a, b, (((1,), (0,)), ((), ())), preferred_element_type=F32)


def iota(shape, dim):
    return lax.broadcasted_iota(jnp.int32, shape, dim).astype(F32)


def whole_part(x, divisor):
    return jnp.floor((x + 0.5) * (1.0 / divisor))


def padded(scratch, array, width):
    rows, used = array.shape
    scratch[0:rows, 0:width] = jnp.zeros((rows, width), F32)
    scratch[0:rows, 0:used] = array.astype(F32)
    return scratch[0:rows, 0:width]


def rotated(frames, points, width, back):
    lane = iota((ROWS, width), 1)
    place = lane - 3.0 * whole_part(lane, 3)
    total = jnp.zeros((ROWS, width), F32)
    for step in range(-2, 3):
        factor = jnp.zeros((ROWS, width), F32)
        for a in range(3):
            b = a + step
            if 0 <= b < 3:
                at = 3 * b + a if back else 3 * a + b
                factor = jnp.where(place == float(a), frames[:, at : at + 1], factor)
        moved = points if step == 0 else pltpu.roll(points, (-step) % width, 1)
        total = total + factor * moved
    return total


def shifted(frames, width):
    lane = iota((ROWS, width), 1)
    place = lane - 3.0 * whole_part(lane, 3)
    total = jnp.zeros((ROWS, width), F32)
    for a in range(3):
        total = jnp.where(place == float(a), frames[:, 9 + a : 10 + a], total)
    return jnp.where(lane < 3.0 * H * PQ, total, 0.0)


def feature_heads():
    lane = iota((1, FEATURES), 1)
    heads = whole_part(lane, C)
    points = whole_part(lane - 256.0, 3 * PQ)
    scalars = whole_part(lane - 512.0, C)
    globals_ = whole_part(lane - 704.0, 3 * PV)
    none = jnp.full((1, FEATURES), 99.0, F32)
    heads = jnp.where(lane < 192.0, heads, none)
    heads = jnp.where((lane >= 256.0) & (lane < 400.0), points, heads)
    heads = jnp.where((lane >= 512.0) & (lane < 704.0), scalars, heads)
    return jnp.where((lane >= 704.0) & (lane < 992.0), globals_, heads)


def head_mask():
    row = whole_part(iota((LANES, FEATURES), 0), ROWS)
    return jnp.where(row == feature_heads(), 1.0, 0.0)


def fill_placing(placing):
    lane = iota((LANES, 1), 0)
    for r in range(8):
        place = jnp.full((LANES, 1), -1.0, F32)
        for first, width, base in ((0, 24, 0), (24, 18, 256), (42, 24, 512), (66, 36, 704)):
            inside = (lane >= float(first)) & (lane < float(first + width))
            place = jnp.where(inside, lane + float(base + r * width - first), place)
        at = iota((LANES, FEATURES), 1)
        placing[r * LANES : (r + 1) * LANES, :] = jnp.where(at == place, 1.0, 0.0).astype(BF16)


def per_head(values, heads):
    total = jnp.zeros(heads.shape, F32)
    for h in range(H):
        total = jnp.where(heads == float(h), values[:, h : h + 1], total)
    return total


def softplus_of(x):
    return jnp.log(1.0 + jnp.exp(x))


def lane_heads():
    return whole_part(iota((1, LANES), 1), ROWS)


def fill_weight(expanded, bias_weight):
    row = whole_part(iota((LANES, H), 0), ROWS)
    pick = jnp.where(row == iota((LANES, H), 1), 1.0, 0.0).astype(BF16)
    rows = nn(pick, bias_weight)
    residue = iota((LANES, LANES), 0)
    residue = residue - ROWS * whole_part(residue, ROWS)
    for i in range(ROWS):
        expanded[:, i * LANES : (i + 1) * LANES] = jnp.where(
            residue == float(i), rows, 0.0
        ).astype(BF16)


def residue_masks():
    row = iota((H * ROWS, LANES), 0)
    row = row - ROWS * whole_part(row, ROWS)
    return [jnp.where(row == float(i), 1.0, 0.0).astype(BF16) for i in range(ROWS)]


def expanded_pairs(block, masks):
    pairs = block[0 : H * ROWS, :]
    wide = jnp.concatenate([pairs * m for m in masks], axis=1)
    return jnp.concatenate([wide, jnp.zeros((LANES - H * ROWS, FEATURES), BF16)], axis=0)


def expanded_features(features, mask):
    twice = jnp.concatenate([features, features], axis=0).astype(BF16)
    return jnp.concatenate([twice] * ROWS, axis=0) * mask


def wide_features(block):
    tall = block[H * ROWS :, :].astype(F32)
    return jnp.concatenate([tall[t * ROWS : (t + 1) * ROWS] for t in range(ROWS)], axis=1)


def packed(vectors, points):
    points = pltpu.roll(points, 64, 1)
    return jnp.concatenate(
        [vectors[:, :128], vectors[:, 128:] + points[:, :128], points[:, 128:]], axis=1
    )


def squared_lengths(points):
    lane = iota((LANES, 256), 1)
    row = whole_part(iota((LANES, 256), 0), ROWS)
    hit = (whole_part(lane, 3 * PQ) == row) & (lane < 3.0 * H * PQ)
    pick = jnp.where(hit, 1.0, 0.0).astype(BF16)
    points = points.astype(BF16).astype(F32)
    squares = points * points
    high = squares.astype(BF16).astype(F32)
    parts = jnp.concatenate(
        [expanded_features(high, pick), expanded_features(squares - high, pick)], axis=1
    )
    total = nt(jnp.ones((ROWS, 512), BF16), parts)
    first = total.astype(BF16).astype(F32)
    second = (total - first).astype(BF16).astype(F32)
    third = (total - first - second).astype(BF16).astype(F32)
    which = iota((ROWS, LANES), 0)
    rows = jnp.where(which == 0.0, first, jnp.where(which == 1.0, second, third))
    return pltpu.roll(jnp.where(which < 3.0, rows, 0.0), 16, 1)


def make_block(block, queries, qpoints, frames, gscalar, gpair, gpoints, wide, loss):
    f = frames[...]
    q = padded(wide, queries[...], 256)
    points = padded(wide, qpoints[...], 256)
    qg = rotated(f, points, 256, False) + shifted(f, 256)
    gs = padded(wide, gscalar[...], 256) * loss
    gg = rotated(f, padded(wide, gpoints[...], 384) * loss, 384, False)
    gg = pltpu.roll(gg, 64, 1)
    lengths = squared_lengths(qg)
    tiles = [q[:, :128], q[:, 128:], qg[:, :128], qg[:, 128:] + lengths, gs[:, :128]]
    tiles += [gs[:, 128:] + gg[:, :128], gg[:, 128:256], gg[:, 256:]]
    pairs = gpair[...].astype(F32) * loss
    tall = [pairs[:, h * CZ : (h + 1) * CZ] for h in range(H)]
    block[...] = jnp.concatenate(tall + tiles, axis=0).astype(BF16)


def make_key_piece(piece, keyset, kpoints, values, vpoints, tall):
    at = 0
    tall[...] = jnp.zeros_like(tall)
    for array in (keyset, kpoints, values, vpoints):
        tall[at : at + array.shape[0], :] = array[...].astype(F32)
        at += array.shape[0]
    piece[...] = tall[...].T.astype(BF16)


def gray(i):
    return i + (i // 2) * (1 - 2 * (i % 2))


def ring_slots(e, z, y):
    s, i = (e + 2) // 4, (e + 2) % 4
    turn = s // 4 + (4 - s) // 4
    low = ((z + 8 - s) % 8) * 4 + (y + gray(i)) % 4
    high = ((z + s) % 8) * 4 + (y + gray((i + 2 * turn) % 4)) % 4
    return low, high


def near_slot(n, z, y):
    m, i = n // 4, n % 4
    dz = ((m + 1) // 2) * (2 * (m % 2) - 1)
    return ((z + 8 + dz) % 8) * 4 + (y + gray(i)) % 4


def forward_groups(pairs, blocks, masks, mask, expanded, keys, square, masking, gamma):
    rows = keys.shape[0]
    biases = nt(jnp.concatenate(pairs, axis=0), expanded[...])
    outs = []
    for k, block in enumerate(blocks):
        features = wide_features(block)
        wide = expanded_features(features, mask[...])
        bias = biases[k * rows : (k + 1) * rows, :]
        dots = nt(keys[:, 0:256], wide[:, 0:256])
        cross = nt(keys[:, 256:512], wide[:, 256:512])
        grads = nt(keys[:, 512:1024], wide[:, 512:1024]) + nt(
            pairs[k], expanded_pairs(block, masks)
        )
        line = features[0:1, 384:512] + features[1:2, 384:512] + features[2:3, 384:512]
        query_square = pltpu.roll(line, LANES - 16, 1)
        distance = query_square + square[...] - 2.0 * cross
        scores = WL * (dots * 0.25 + bias) - (DIST_WEIGHT * gamma) * distance - masking
        top = jnp.max(scores, axis=0, keepdims=True)
        weights = jnp.exp(scores - top)
        total = jnp.sum(weights, axis=0, keepdims=True)
        inner = jnp.sum(weights * grads, axis=0, keepdims=True)
        outs.append((weights, grads, distance, top, total, inner))
    return outs


def combine_stats(arrived, answers, table):
    for d in range(32):
        for n in range(3):
            table[n, d : d + 1, :] = arrived[d, :, n * LANES : (n + 1) * LANES]
    tops = table[0]
    top = jnp.max(tops, axis=0, keepdims=True)
    factors = jnp.exp(tops - top)
    total = jnp.sum(factors * table[1], axis=0, keepdims=True)
    inner = jnp.sum(factors * table[2], axis=0, keepdims=True) / total
    factors = factors / total
    for d in range(32):
        answers[d, :, 0:LANES] = factors[d : d + 1, :]
        answers[d, :, LANES : 2 * LANES] = inner


def score_group(factor, inner, weights, grads, distance):
    probs = weights * factor
    score = probs * (grads - inner)
    head_part = jnp.sum(score * distance, axis=0, keepdims=True)
    return (WL * score).astype(BF16), probs.astype(BF16), head_part


def bias_group(score_half, pairs, flipped):
    turned = score_half.astype(F32).T
    flipped[...] = turned
    bias_part = jnp.zeros((16, LANES), F32)
    for i in range(ROWS):
        rows = flipped[pl.ds(i, 16, stride=ROWS), :].astype(BF16)
        bias_part = bias_part + nn(rows, pairs[i])
    return turned.astype(BF16), bias_part


def query_group(turned, features, head_rows, packed_keys, scale, point_scale):
    product = nn(turned, packed_keys)
    row_sum = jnp.sum(turned.astype(F32), axis=1, keepdims=True)
    query_part = jnp.zeros((ROWS, 384), F32)
    row_part = jnp.zeros((ROWS, 256), F32)
    for h in range(H):
        at = slice(h * ROWS, (h + 1) * ROWS)
        query_part = query_part + head_rows[at, 0:384] * product[at, :]
        row_part = row_part + head_rows[at, 384:640] * row_sum[at, :]
    less = point_scale * pltpu.roll(features[:, 256:512], 64, 1) * row_part
    query_part = scale * query_part
    return jnp.concatenate([query_part[:, :128], query_part[:, 128:] - less], axis=1)


def sum_of(ref, count):
    total = ref[0].astype(F32)
    for k in range(1, count):
        total = total + ref[k].astype(F32)
    return total


def main_kernel(
    loss,
    residues,
    pair_hbm,
    queries_hbm,
    qpoints_hbm,
    frames_hbm,
    keyset_hbm,
    kpoints_hbm,
    values_hbm,
    vpoints_hbm,
    key_mask_hbm,
    weight_hbm,
    head_weight_hbm,
    gscalar_hbm,
    gpair_hbm,
    gpoints_hbm,
    pair_out,
    query_hbm,
    key_hbm,
    total_hbm,
    queries,
    qpoints,
    frames,
    keyset,
    kpoints,
    values,
    vpoints,
    key_mask,
    weight,
    head_weight,
    gscalar,
    gpair,
    gpoints,
    pair,
    blocks,
    own_block,
    pieces,
    own_piece,
    piece_rows,
    wide,
    mask,
    head_rows,
    expanded,
    placing,
    keys,
    packed_keys,
    square,
    weights,
    grads,
    distance,
    stats,
    arrived,
    answers,
    answered,
    table,
    halves,
    query_out,
    key_out,
    total_out,
    pair_stage,
    turned,
    flipped,
    key_acc,
    sum_acc,
    bias_acc,
    head_acc,
    query_parts,
    query_in,
    key_parts,
    key_in,
    totals,
    row_in,
    y_in,
    z_in,
    small_sem,
    input_sem,
    pair_sem,
    own_sem,
    out_sem,
    send_sem,
    upper_recv,
    lower_recv,
    key_send,
    key_recv,
    stats_send,
    stats_recv,
    answer_send,
    answer_recv,
    query_send,
    query_recv,
    part_send,
    part_recv,
    total_send,
    total_recv,
):
    row, col = lax.axis_index("row"), lax.axis_index("col")
    z, y = col // 4, col % 4
    here = (row, col)
    groups = blocks.shape[0]

    def remote(source, target, send, recv, device):
        return pltpu.make_async_remote_copy(source, target, send, recv, device, MESH)

    barrier = pltpu.get_barrier_semaphore()
    for d in (1, 2, 3):
        pl.semaphore_signal(barrier, 1, device_id=(row, z * 4 + (y + d) % 4), device_id_type=MESH)
    for d in (1, 7):
        pl.semaphore_signal(
            barrier, 1, device_id=(row, ((z + d) % 8) * 4 + y), device_id_type=MESH
        )
    for d in range(1, 8):
        pl.semaphore_signal(barrier, 1, device_id=((row + d) % 8, col), device_id_type=MESH)
    inputs = (
        (queries_hbm, queries),
        (qpoints_hbm, qpoints),
        (frames_hbm, frames),
        (keyset_hbm, keyset),
        (kpoints_hbm, kpoints),
        (values_hbm, values),
        (vpoints_hbm, vpoints),
        (key_mask_hbm, key_mask),
        (weight_hbm, weight),
        (head_weight_hbm, head_weight),
        (gscalar_hbm, gscalar),
        (gpair_hbm, gpair),
        (gpoints_hbm, gpoints),
    )
    input_copies = []
    for k, (source, target) in enumerate(inputs):
        copy = pltpu.make_async_copy(source, target, input_sem.at[k])
        copy.start()
        input_copies.append(copy)
    quarter = pair.shape[0] // 4
    pair_copies = []
    for k in range(4):
        at = pl.ds(k * quarter, quarter)
        copy = pltpu.make_async_copy(pair_hbm.at[at], pair.at[at], pair_sem.at[k])
        copy.start()
        pair_copies.append(copy)
    for copy in input_copies:
        copy.wait()
    make_block(own_block, queries, qpoints, frames, gscalar, gpair, gpoints, wide, loss)
    make_key_piece(own_piece, keyset, kpoints, values, vpoints, piece_rows)
    pl.semaphore_wait(barrier, 12)

    up = (row, ((z + 1) % 8) * 4 + y)
    down = (row, ((z + 7) % 8) * 4 + y)

    parts = ((pl.ds(0, 160), upper_recv),)

    def send_part(source, slot, target, part):
        at, recv = part
        remote(source.at[at], blocks.at[slot, at], send_sem, recv.at[slot], target).start()

    def part_arrived(slot, part):
        at, recv = part
        remote(own_block.at[at], blocks.at[slot, at], send_sem, recv.at[slot], here).wait_recv()

    for part in parts:
        send_part(own_block, col, up, part)
        send_part(own_block, col, down, part)
        for d in (1, 3, 2):
            send_part(own_block, col, (row, z * 4 + (y + d) % 4), part)
    for d in range(1, 8):
        peer = ((row + d) % 8, col)
        remote(own_piece, pieces.at[row], key_send.at[d], key_recv.at[row], peer).start()
    own_copy = pltpu.make_async_copy(own_block, blocks.at[col], own_sem.at[0])
    own_copy.start()
    piece_copy = pltpu.make_async_copy(own_piece, pieces.at[row], own_sem.at[1])
    piece_copy.start()

    full = head_mask()
    mask[...] = full.astype(BF16)
    head_rows[:, 0:384] = packed(full[0 : H * ROWS, 0:256], full[0 : H * ROWS, 256:512])
    head_rows[:, 384:640] = pltpu.roll(full[0 : H * ROWS, 256:512], 64, 1)
    fill_weight(expanded, weight[...])
    fill_placing(placing)
    key_acc[...] = jnp.zeros_like(key_acc)
    sum_acc[...] = jnp.zeros_like(sum_acc)
    bias_acc[...] = jnp.zeros_like(bias_acc)
    head_acc[...] = jnp.zeros_like(head_acc)
    masks = residue_masks()
    gamma = softplus_of(per_head(head_weight, lane_heads()))
    point_gamma = softplus_of(per_head(head_weight, feature_heads()[:, 256:512]))
    vector_scale = jnp.where(iota((1, 256), 1) < 1.0 * H * C, 0.25, 0.0)
    used = jnp.where(iota((1, 256), 1) < 3.0 * H * PQ, WC * point_gamma, 0.0)
    scale = packed(vector_scale, used)
    point_scale = pltpu.roll(used, 64, 1)
    masking = 100000.0 * (1.0 - key_mask[...].astype(F32))
    masking = jnp.broadcast_to(masking, (ROWS, masking.shape[1])).T[:, 0:1]

    for d in (1, 3, 2):
        slot = z * 4 + (y + d) % 4
        for part in parts:
            part_arrived(slot, part)
            send_part(blocks.at[slot], slot, up, part)
            send_part(blocks.at[slot], slot, down, part)
    for d in range(1, 8):
        source = (row + d) % 8
        remote(own_piece, pieces.at[source], key_send.at[d], key_recv.at[source], here).wait_recv()
    piece_copy.wait()
    own_copy.wait()
    tall = jnp.concatenate([pieces[r] for r in range(8)], axis=1)
    keys[...] = nn(tall, placing[...]).astype(BF16)
    points = keys[:, 256:512].astype(F32)
    packed_keys[...] = packed(keys[:, 0:256].astype(F32), points).astype(BF16)
    squares = points * points
    high_part = squares.astype(BF16)
    low_part = (squares - high_part.astype(F32)).astype(BF16)
    square[...] = nt(high_part, mask[:, 256:512]) + nt(low_part, mask[:, 256:512])
    for copy in pair_copies:
        copy.wait()

    def send_stats(slot):
        remote(
            stats.at[slot], arrived.at[col], stats_send, stats_recv, (row, slot)
        ).start()

    def pairs_of(slot):
        first = pl.multiple_of(slot * ROWS, ROWS)
        return [pair[first + i] for i in range(ROWS)]

    def forward_two(slots):
        pairs = [jnp.concatenate(pairs_of(slot), axis=1) for slot in slots]
        outs = forward_groups(
            pairs,
            [blocks[slot] for slot in slots],
            masks,
            mask,
            expanded,
            keys,
            square,
            masking,
            gamma,
        )
        for slot, out in zip(slots, outs):
            weights[slot], grads[slot], distance[slot] = out[0], out[1], out[2]
            for n in range(3):
                stats[slot, :, n * LANES : (n + 1) * LANES] = out[3 + n]

    def forward_step(e, _):
        low, high = ring_slots(e, z, y)

        for part in parts:

            @pl.when(e >= 2)
            def _(part=part):
                part_arrived(low, part)

            @pl.when((e >= 2) & (e <= 11))
            def _(part=part):
                send_part(blocks.at[low], low, up, part)

            @pl.when(e >= 2)
            def _(part=part):
                part_arrived(high, part)

            @pl.when(((e >= 2) & (e <= 9)) | ((e >= 12) & (e <= 13)))
            def _(part=part):
                send_part(blocks.at[high], high, down, part)

        @pl.when(e >= 1)
        def _():
            send_stats(ring_slots(e - 1, z, y)[0])

        @pl.when(e >= 2)
        def _():
            send_stats(ring_slots(e - 1, z, y)[1])

        forward_two((low, high))
        return 0

    lax.fori_loop(0, 16, forward_step, 0)
    arrived[col] = stats[col]
    for slot in ring_slots(15, z, y):
        send_stats(slot)

    most = pl.ds(0, groups - 1)

    def all_of(buffer, sem):
        pltpu.make_async_copy(buffer.at[most], buffer.at[most], sem).wait()

    all_of(arrived, stats_recv)
    combine_stats(arrived, answers, table)

    for d in range(16, 48):
        if d != 32:
            peer = (col + d) % 32
            remote(
                answers.at[peer],
                answered.at[col],
                answer_send,
                answer_recv.at[col],
                (row, peer),
            ).start()
    answered[col] = answers[col]

    def score_one(slot, k):
        pairs = pairs_of(slot)
        score_half, probs_half, head_part = score_group(
            answered[slot, :, 0:LANES],
            answered[slot, :, LANES : 2 * LANES],
            weights[slot],
            grads[slot],
            distance[slot],
        )
        halves[slot, :, 0:LANES] = score_half
        halves[slot, :, LANES : 2 * LANES] = probs_half
        turned[slot], bias_part = bias_group(score_half, pairs, flipped.at[k])
        return bias_part, head_part

    def answer_arrived(slot):
        remote(
            answers.at[slot], answered.at[slot], answer_send, answer_recv.at[slot], here
        ).wait_recv()

    def score_step(e, _):
        slots = [near_slot(4 * e + k, z, y) for k in range(4)]

        @pl.when(e >= 1)
        def _():
            answer_arrived(slots[0])

        for slot in slots[1:]:
            answer_arrived(slot)
        parts = [score_one(slot, k) for k, slot in enumerate(slots)]
        bias_acc[...] += (parts[0][0] + parts[1][0]) + (parts[2][0] + parts[3][0])
        head_acc[...] += (parts[0][1] + parts[1][1]) + (parts[2][1] + parts[3][1])
        return 0

    lax.fori_loop(0, 8, score_step, 0)
    totals[0, :, :] = bias_acc[...]
    totals[0, H : H + 1, :] = head_acc[...]

    def spread_total(source, target, me, count, base, device):
        for d in range(1, count):
            remote(
                source,
                target.at[me],
                total_send.at[base + d],
                total_recv.at[base + me],
                device((me + d) % count),
            ).start()

    def total_arrived(source, target, me, count, base):
        for d in range(1, count):
            peer = (me + d) % count
            remote(
                source, target.at[peer], total_send.at[base + d], total_recv.at[base + peer], here
            ).wait_recv()

    spread_total(totals.at[0], row_in, row, 8, 0, lambda p: (p, col))
    row_in[row] = totals[0]

    def send_query(slot):
        remote(
            query_parts.at[slot], query_in.at[col], query_send, query_recv, (row, slot)
        ).start()

    def small_two(slots):
        wides = []
        for slot in slots:
            features = wide_features(blocks[slot])
            wides.append(expanded_features(features, mask[...]))
            query_parts[slot] = query_group(
                turned[slot], features, head_rows, packed_keys[...], scale, point_scale
            ).astype(BF16)
        wide = jnp.concatenate(wides, axis=0)
        scores = [halves[slot, :, 0:LANES] for slot in slots]
        probs = [halves[slot, :, LANES : 2 * LANES] for slot in slots]
        key_acc[:, 0:512] += nn(jnp.concatenate(scores, axis=1), wide[:, 0:512])
        key_acc[:, 512:1024] += nn(jnp.concatenate(probs, axis=1), wide[:, 512:1024])
        sum_acc[...] += scores[0].astype(F32) + scores[1].astype(F32)

    def small_step(e, _):
        first, second = near_slot(31 - 2 * e, z, y), near_slot(30 - 2 * e, z, y)

        @pl.when(e >= 1)
        def _():
            send_query(near_slot(33 - 2 * e, z, y))
            send_query(near_slot(32 - 2 * e, z, y))

        small_two((first, second))
        return 0

    def stage_copy(slot):
        at = pl.ds(pl.multiple_of(slot * ROWS, ROWS), ROWS)
        return pltpu.make_async_copy(pair_stage.at[at], pair_out.at[at], out_sem)

    def pair_step(e, _):
        @pl.when(e >= 1)
        def _():
            stage_copy(2 * e - 2).start()
            stage_copy(2 * e - 1).start()

        for k in range(2):
            slot = 2 * e + k
            first = pl.multiple_of(slot * ROWS, ROWS)
            side = jnp.concatenate([expanded[...], expanded_pairs(blocks[slot], masks)], axis=0)
            out = nn(halves[slot], side)
            for i in range(ROWS):
                pair_stage[first + i] = out[:, i * LANES : (i + 1) * LANES].astype(BF16)
        return 0

    lax.fori_loop(0, 8, small_step, 0)
    lax.fori_loop(0, 2, pair_step, 0)
    total_arrived(totals.at[0], row_in, row, 8, 0)
    totals[1] = sum_of(row_in, 8)
    y_in[y] = totals[1]
    spread_total(totals.at[1], y_in, y, 4, 8, lambda p: (row, z * 4 + p))
    lax.fori_loop(8, 16, small_step, 0)
    send_query(near_slot(1, z, y))
    query_in[col] = query_parts[col]
    total_arrived(totals.at[1], y_in, y, 4, 8)
    totals[2] = sum_of(y_in, 4)
    z_in[z] = totals[2]
    spread_total(totals.at[2], z_in, z, 8, 12, lambda p: (row, p * 4 + y))
    sum_high = sum_acc[...].astype(BF16)
    sum_low = (sum_acc[...] - sum_high.astype(F32)).astype(BF16)
    key_sum = nn(sum_high, mask[:, 256:512]) + nn(sum_low, mask[:, 256:512])
    key_points = (WC * point_gamma) * (
        key_acc[:, 256:512] - keys[:, 256:512].astype(F32) * key_sum
    )
    whole = jnp.concatenate(
        [0.25 * key_acc[:, 0:256], key_points, key_acc[:, 512:1024]], axis=1
    ).astype(BF16)
    spread = nt(whole, placing[...])
    for r in range(8):
        key_parts[r] = spread[:, r * LANES : (r + 1) * LANES].astype(BF16)
    key_in[row] = key_parts[row]
    for d in range(1, 8):
        peer = (row + d) % 8
        remote(
            key_parts.at[peer], key_in.at[row], part_send.at[d], part_recv.at[row], (peer, col)
        ).start()

    lax.fori_loop(2, 16, pair_step, 0)

    all_of(query_in, query_recv)
    mine = sum_of(query_in, 32)
    query_out[:, 0:256] = mine[:, 0:256]
    back = pltpu.roll(mine, 384 - 192, 1)[:, 0:256]
    lane = iota((ROWS, 256), 1)
    back = jnp.where(lane < 3.0 * H * PQ, back, 0.0)
    query_out[:, 256:512] = rotated(frames[...], back, 256, True)
    stage_copy(groups - 2).start()
    stage_copy(groups - 1).start()
    for d in range(1, 8):
        peer = (row + d) % 8
        remote(
            key_parts.at[peer], key_in.at[peer], part_send.at[d], part_recv.at[peer], here
        ).wait_recv()
    key_out[...] = sum_of(key_in, 8).T
    small_copies = [
        pltpu.make_async_copy(query_out, query_hbm, small_sem.at[0]),
        pltpu.make_async_copy(key_out, key_hbm, small_sem.at[1]),
        pltpu.make_async_copy(total_out, total_hbm, small_sem.at[2]),
    ]
    small_copies[0].start()
    total_arrived(totals.at[2], z_in, z, 8, 12)
    small_copies[1].start()
    total_out[...] = sum_of(z_in, 8)

    all_of(blocks, send_sem)
    for d in range(1, 8):
        remote(own_piece, pieces.at[0], key_send.at[d], key_recv.at[0], here).wait_send()
        remote(key_parts.at[0], key_in.at[0], part_send.at[d], part_recv.at[0], here).wait_send()

    all_of(arrived, stats_send)
    all_of(answers, answer_send)
    all_of(query_in, query_send)
    for base, count in ((0, 8), (8, 4), (12, 8)):
        for d in range(1, count):
            remote(
                totals.at[0], row_in.at[0], total_send.at[base + d], total_recv.at[0], here
            ).wait_send()

    small_copies[2].start()
    pltpu.make_async_copy(pair_stage, pair_out, out_sem).wait()
    for copy in small_copies:
        copy.wait()


def last_kernel(residues, *refs):
    pair_in, head_hbm, query_hbm, key_hbm, total_hbm = refs[:5]
    pair_grad, *outs = refs[5:14]
    stage, head_weight, query_sum, key_sum, total_sum, *finals = refs[14:27]
    in_sem, out_sem, small_in, small_out = refs[27:]
    pieces = in_sem.shape[0]
    size = stage.shape[0] // pieces
    arrivals, leaves = [], []
    smalls = (
        (head_hbm, head_weight),
        (query_hbm, query_sum),
        (key_hbm, key_sum),
        (total_hbm, total_sum),
    )
    small_copies = [
        pltpu.make_async_copy(source, target, small_in.at[k])
        for k, (source, target) in enumerate(smalls)
    ]
    for k in range(pieces):
        at = pl.ds(k * size, size)
        arrivals.append(pltpu.make_async_copy(pair_in.at[at], stage.at[at], in_sem.at[k]))
        leaves.append(pltpu.make_async_copy(stage.at[at], pair_grad.at[at], out_sem.at[k]))
        arrivals[k].start()
        if k < len(small_copies):
            small_copies[k].start()
    for copy in small_copies:
        copy.wait()
    queries_grad, qpoints_grad, *turned, bias_grad, head_grad = finals
    queries_grad[...] = query_sum[:, 0:192]
    qpoints_grad[...] = query_sum[:, 256:400]
    at = 0
    for out in turned:
        out[...] = key_sum[at : at + out.shape[0], :]
        at += out.shape[0]
    bias_grad[...] = total_sum[0:H, :] * (1.0 / residues)
    heads = lane_heads()
    raw = per_head(head_weight, heads)
    line = total_sum[H : H + 1, :] * (-DIST_WEIGHT / residues) / (1.0 + jnp.exp(-raw))
    lane = iota((1, LANES), 1)
    total = jnp.zeros((1, LANES), F32)
    for h in range(H):
        part = jnp.sum(jnp.where(heads == float(h), line, 0.0), axis=1, keepdims=True)
        total = jnp.where(lane == float(h), part, total)
    head_grad[...] = total[:, 0:H]
    for k in range(pieces):
        arrivals[k].wait()
        leaves[k].start()
    for k, (source, target) in enumerate(zip(finals, outs)):
        copy = pltpu.make_async_copy(source, target, small_out.at[k])
        copy.start()
        leaves.append(copy)
    for copy in leaves:
        copy.wait()


def shape(*dims, dtype=F32):
    return jax.ShapeDtypeStruct(dims, dtype)


VMEM = pl.BlockSpec(memory_space=pltpu.VMEM)
SMEM = pl.BlockSpec(memory_space=pltpu.SMEM)
ANY = pl.BlockSpec(memory_space=pl.ANY)
HBM = pl.BlockSpec(memory_space=pltpu.HBM)
DMA = pltpu.SemaphoreType.DMA


def local(
    pair_rep,
    queries,
    qpoints,
    frames,
    keyset,
    kpoints,
    values,
    vpoints,
    key_mask,
    bias_weight,
    head_weight,
    grad_scalar,
    grad_pair,
    grad_points,
):
    rows, keys, _ = pair_rep.shape
    residues = queries.shape[0] * 256
    loss = float(residues // 16)
    groups = rows // ROWS
    weight = bias_weight.T
    full, half = pltpu.VMEM, lambda *dims: pltpu.VMEM(dims, BF16)
    given = (
        queries,
        qpoints,
        frames,
        keyset.T,
        kpoints.T,
        values.T,
        vpoints.T,
        key_mask.reshape(1, keys),
        weight,
        head_weight.reshape(1, H),
        grad_scalar,
        grad_pair,
        grad_points,
    )
    pair_main, query_sum, key_sum, total_sum = pl.pallas_call(
        functools.partial(main_kernel, loss, float(residues)),
        out_shape=(
            shape(rows, keys, LANES, dtype=BF16),
            shape(ROWS, 512),
            shape(LANES, keys),
            shape(16, LANES),
        ),
        in_specs=[HBM] * (1 + len(given)),
        out_specs=(HBM,) * 4,
        scratch_shapes=[
            *(full(array.shape, array.dtype) for array in given),
            half(rows, keys, LANES),
            half(groups, 160, LANES),
            half(160, LANES),
            half(8, keys, LANES),
            half(keys, LANES),
            full((LANES, keys), F32),
            full((ROWS, 384), F32),
            half(LANES, FEATURES),
            full((H * ROWS, 640), F32),
            half(LANES, FEATURES),
            half(FEATURES, FEATURES),
            half(keys, FEATURES),
            half(keys, 384),
            full((keys, LANES), F32),
            full((groups, keys, LANES), F32),
            full((groups, keys, LANES), F32),
            full((groups, keys, LANES), F32),
            full((groups, 1, 3 * LANES), F32),
            full((groups, 1, 3 * LANES), F32),
            full((groups, 1, 2 * LANES), F32),
            full((groups, 1, 2 * LANES), F32),
            full((3, groups, LANES), F32),
            half(groups, keys, 2 * LANES),
            full((ROWS, 512), F32),
            full((LANES, keys), F32),
            full((16, LANES), F32),
            half(rows, keys, LANES),
            half(groups, LANES, keys),
            full((4, LANES, keys), F32),
            full((keys, FEATURES), F32),
            full((keys, LANES), F32),
            full((16, LANES), F32),
            full((1, LANES), F32),
            half(groups, ROWS, 384),
            half(groups, ROWS, 384),
            half(8, keys, LANES),
            half(8, keys, LANES),
            full((3, 16, LANES), F32),
            full((8, 16, LANES), F32),
            full((4, 16, LANES), F32),
            full((8, 16, LANES), F32),
            DMA((3,)),
            DMA((len(given),)),
            DMA((4,)),
            DMA((2,)),
            DMA,
            DMA,
            DMA((groups,)),
            DMA((groups,)),
            DMA((8,)),
            DMA((8,)),
            DMA,
            DMA,
            DMA,
            DMA((groups,)),
            DMA,
            DMA,
            DMA((8,)),
            DMA((8,)),
            DMA((20,)),
            DMA((20,)),
        ],
        compiler_params=pltpu.CompilerParams(
            collective_id=0, has_side_effects=True, vmem_limit_bytes=67043328
        ),
        name="main",
    )(pair_rep, *given)
    finals = (
        (ROWS, H * C),
        (ROWS, 3 * H * PQ),
        (24, keys),
        (18, keys),
        (24, keys),
        (36, keys),
        (H, CZ),
        (1, H),
    )
    pair_grad, queries_grad, qpoints_grad, *turned, bias_grad, head_grad = pl.pallas_call(
        functools.partial(last_kernel, float(residues)),
        out_shape=(
            shape(rows, keys, LANES, dtype=BF16),
            *(shape(*dims) for dims in finals),
        ),
        in_specs=[HBM] * 5,
        out_specs=(HBM,) * 9,
        scratch_shapes=[
            half(rows, keys, LANES),
            full((1, H), F32),
            full((ROWS, 512), F32),
            full((LANES, keys), F32),
            full((16, LANES), F32),
            *(full(dims, F32) for dims in finals),
            DMA((8,)),
            DMA((8,)),
            DMA((4,)),
            DMA((8,)),
        ],
        compiler_params=pltpu.CompilerParams(vmem_limit_bytes=67043328),
        name="last",
    )(pair_main, head_weight.reshape(1, H), query_sum, key_sum, total_sum)
    return (
        pair_grad,
        queries_grad,
        qpoints_grad,
        *(array.T for array in turned),
        bias_grad.T,
        head_grad.reshape(H),
    )


def solution(mesh):
    both = ("row", "col")
    return jax.shard_map(
        local,
        mesh=mesh,
        in_specs=(
            P("row", "col", None),
            P(both, None),
            P(both, None),
            P(both, None),
            P("col", "row"),
            P("col", "row"),
            P("col", "row"),
            P("col", "row"),
            P("col"),
            P(),
            P(),
            P(both, None),
            P(both, None),
            P(both, None),
        ),
        out_specs=(
            P("row", "col", None),
            P(both, None),
            P(both, None),
            P("col", "row"),
            P("col", "row"),
            P("col", "row"),
            P("col", "row"),
            P(),
            P(),
        ),
        check_vma=False,
    )
```
